32 devices in a mesh: gx: 4 (over y, x), gy: 4 (over z), gz: 2 (over core).
Axes of the slice: x: 2, y: 2, z: 4, core: 2. Of those that a mesh axis runs over, the one named last changes fastest.
Arguments:
- position: float32 [4096, 3, 128], P(('gx', 'gy', 'gz')), may hold values from 0 to 4, as said below
- velocity: float32 [4096, 3, 128], P(('gx', 'gy', 'gz')), may hold values from -0.3 to 0.3
- particle_mass: float32 [4096, 128], P(('gx', 'gy', 'gz')), may hold values from 0.001953125 to 0.0078125
- send_first: int32 [32, 32, 4], P(('gx', 'gy', 'gz')), may hold values from -1 to 127, as said below
- neighbours_first: int32 [4096, 16], P(('gx', 'gy', 'gz')), may hold values from 0 to 255, as said below
- destination: int32 [4096], P(('gx', 'gy', 'gz')), may hold values from 0 to 4095, as said below
- send_second: int32 [32, 32, 4], P(('gx', 'gy', 'gz')), may hold values from -1 to 127, as said below
- neighbours_second: int32 [4096, 16], P(('gx', 'gy', 'gz')), may hold values from 0 to 255, as said below
Outputs:
- position_out: float32 [4096, 3, 128], P(('gx', 'gy', 'gz'))
- velocity_out: float32 [4096, 3, 128], P(('gx', 'gy', 'gz'))
- density_out: float32 [4096, 128], P(('gx', 'gy', 'gz'))
The draws below stay inside these ranges and needn't reach their ends.
Inputs may be any that keep to these rules, and one draw needn't show every extreme that they name: The particles of a block owned by the device at grid position (i_gx, i_gy, i_gz) lie in its box [i_gx, i_gx + 1] x [i_gy, i_gy + 1] x [i_gz, i_gz + 1], all of one block within a cube of side 1/2. `send_first`: only devices whose grid positions along gx, gy and gz differ by at most one in each (and are not the same) send ghosts to each other. The filled slots of one pair come first and hold distinct blocks; some pair fills all 4 slots. `send_second`: as for send_first, in the new layout. `neighbours_first`: entries name only the device's own blocks or filled ghost slots of send_first; the entries of a block are distinct and never the block itself. `neighbours_second`: entries name only the device's own blocks or filled ghost slots of send_second; the entries of a block are distinct and never the block itself. `destination`: A permutation of the 4096 positions; a block stays or moves to a device next to its owner along exactly one of gx, gy, gz; at most 2 blocks go from one device to another, and some pairs move exactly 2.
All inputs are finite; a program needn't handle non-finite values.
Results may differ from the reference program's by a relative error of at most 0.0001.
Values sent between devices are 32-bit elements; how exact they have to be, the bound alone decides.
A program may use at most 128 MiB of HBM per device.

```python
import math
import jax
import jax.numpy as jnp
from jax import lax

PARTICLES = 128
NEIGHBOURS = 16
BLOCKS = 128
GHOST_CAP = 4
MOVE_CAP = 2
ALL_BLOCKS = 4096
N_GX = 4
N_GY = 4
N_GZ = 2


def grid_places():
    devices = N_GX * N_GY * N_GZ
    index = jnp.arange(devices, dtype=jnp.int32)
    along = (index // (N_GY * N_GZ), index // N_GZ % N_GY, index % N_GZ)
    return (index, along)


def block_cells(key):
    index, along = grid_places()
    devices = N_GX * N_GY * N_GZ
    scores = jax.random.randint(jax.random.fold_in(key, 21), (devices, BLOCKS), 0, 1 << 14) * BLOCKS
    ordered = jnp.argsort(scores + jnp.arange(BLOCKS, dtype=jnp.int32)[None, :], axis=1).astype(jnp.int32)
    octant = ordered % 8
    first = 2 * along[0][:, None] + octant // 4
    second = 2 * along[1][:, None] + octant // 2 % 2
    third = 2 * along[2][:, None] + octant % 2
    return jnp.stack([first, second, third], axis=2).astype(jnp.int32)


def draw_destination(key, part):
    base = jax.random.fold_in(key, 13)
    index, along = grid_places()
    devices = N_GX * N_GY * N_GZ
    extents = (N_GX, N_GY, N_GZ)
    strides = (N_GY * N_GZ, N_GZ, 1)
    cells = block_cells(key)
    block_index = jnp.arange(BLOCKS, dtype=jnp.int32)
    target = index[:, None] * BLOCKS + block_index[None, :]
    taken = jnp.zeros((devices, BLOCKS), jnp.int32)
    for rounds in range(6):
        axis_number = rounds // 2
        parity = rounds % 2
        place = along[axis_number]
        partner_place = jnp.where((place - parity) % 2 == 0, place + 1, place - 1)
        exists = (partner_place >= 0) & (partner_place < extents[axis_number])
        partner = jnp.clip(index + (partner_place - place) * strides[axis_number], 0, devices - 1)
        local_cell = cells[:, :, axis_number] - 2 * place[:, None]
        facing = jnp.where((partner_place > place)[:, None], local_cell == 1, local_cell == 0)
        ranking = jax.random.randint(jax.random.fold_in(base, 20 + rounds), (devices, BLOCKS), 0, 1 << 14) * BLOCKS
        ranking = ranking + block_index[None, :] + jnp.where(facing, 0, 1 << 28) + taken * (1 << 29)
        picked = jnp.argsort(ranking, axis=1).astype(jnp.int32)[:, :MOVE_CAP]
        amount = jax.random.randint(jax.random.fold_in(base, rounds + 1), (devices,), 1, MOVE_CAP + 1)
        if rounds == 0:
            amount = jnp.full((devices,), MOVE_CAP, jnp.int32)
        pair_amount = amount[jnp.minimum(index, partner)]
        for offset in range(MOVE_CAP):
            mine = picked[:, offset]
            theirs = picked[partner, offset]
            active = exists & (offset < pair_amount)
            target = target.at[index, mine].set(jnp.where(active, partner * BLOCKS + theirs, target[index, mine]))
            taken = taken.at[index, mine].set(jnp.maximum(taken[index, mine], active.astype(jnp.int32)))
    return target.reshape(devices * BLOCKS).astype(jnp.int32)


def moved_cells(key):
    cells = block_cells(key)
    devices = N_GX * N_GY * N_GZ
    destination = draw_destination(key, 0)
    flat = jnp.zeros((devices * BLOCKS, 3), jnp.int32).at[destination].set(cells.reshape(devices * BLOCKS, 3))
    return flat.reshape(devices, BLOCKS, 3)


def ghost_tables(key, which, cells):
    base = jax.random.fold_in(key, which)
    index, along = grid_places()
    devices = N_GX * N_GY * N_GZ
    near = (jnp.abs(along[0][:, None] - along[0][None, :]) <= 1) & (jnp.abs(along[1][:, None] - along[1][None, :]) <= 1)
    near = near & (jnp.abs(along[2][:, None] - along[2][None, :]) <= 1) & (index[:, None] != index[None, :])
    corner = jnp.stack(along, axis=1)
    lower = 2 * corner - 1
    upper = 2 * corner + 2
    eligible = (cells[:, None, :, :] >= lower[None, :, None, :]) & (cells[:, None, :, :] <= upper[None, :, None, :])
    eligible = jnp.all(eligible, axis=3)
    reach = jnp.sum(eligible.astype(jnp.int32), axis=2)
    amount = jax.random.randint(jax.random.fold_in(base, 1), (devices, devices), 1, GHOST_CAP + 1)
    forced = (index[:, None] == 1) & (index[None, :] == 0) | (index[:, None] == 0) & (index[None, :] == 1)
    amount = jnp.minimum(jnp.where(forced, GHOST_CAP, amount), reach) * near.astype(jnp.int32)
    block_index = jnp.arange(BLOCKS, dtype=jnp.int32)
    scores = jax.random.randint(jax.random.fold_in(base, 2), (devices, devices, BLOCKS), 0, 1 << 14) * BLOCKS
    scores = scores + block_index[None, None, :] + jnp.where(eligible, 0, 1 << 28)
    chosen = jnp.argsort(scores, axis=2).astype(jnp.int32)[:, :, :GHOST_CAP]
    slot_index = jnp.arange(GHOST_CAP, dtype=jnp.int32)
    sender = jnp.where(slot_index[None, None, :] < amount[:, :, None], chosen, -1).astype(jnp.int32)
    received = jnp.transpose(sender, (1, 0, 2))
    ghost_cell = cells[index[None, :, None], jnp.maximum(received, 0)]
    entry_cells = jnp.concatenate([cells, ghost_cell.reshape(devices, devices * GHOST_CAP, 3)], axis=1)
    filled = jnp.concatenate([jnp.ones((devices, BLOCKS), bool), (received >= 0).reshape(devices, devices * GHOST_CAP)], axis=1)
    width = BLOCKS + devices * GHOST_CAP
    entry_index = jnp.arange(width, dtype=jnp.int32)
    adjacent = filled[:, None, :] & jnp.ones((devices, BLOCKS, width), bool)
    for axis_number in range(3):
        spacing = cells[:, :, None, axis_number] - entry_cells[:, None, :, axis_number]
        adjacent = adjacent & (jnp.abs(spacing) <= 1)
    host_score = jax.random.randint(jax.random.fold_in(base, 3), (devices, BLOCKS, width), 0, 1 << 14) * BLOCKS
    host_score = host_score + block_index[None, :, None] + jnp.where(adjacent, 1 << 28, 0)
    host_block = jnp.argsort(host_score, axis=1).astype(jnp.int32)[:, BLOCKS - 1, :]
    designated = (block_index[None, :, None] == host_block[:, None, :]) & adjacent & (entry_index >= BLOCKS)[None, None, :]
    own_entry = entry_index[None, None, :] == block_index[None, :, None]
    entry_class = jnp.where(designated, 0, jnp.where(adjacent, 1, 2))
    entry_class = jnp.where(jnp.logical_not(filled)[:, None, :], 3, entry_class)
    entry_class = jnp.where(own_entry, 4, entry_class)
    ranking = jax.random.randint(jax.random.fold_in(base, 4), (devices, BLOCKS, width), 0, 1 << 12) * width
    ranking = entry_class * (1 << 26) + ranking + entry_index[None, None, :]
    entries = jnp.argsort(ranking, axis=2).astype(jnp.int32)[:, :, :NEIGHBOURS]
    return (sender, entries.reshape(devices * BLOCKS, NEIGHBOURS).astype(jnp.int32))


def draw_position(key, part):
    devices = N_GX * N_GY * N_GZ
    cells = block_cells(key).reshape(devices * BLOCKS, 3).astype(jnp.float32)
    base = jax.random.fold_in(key, 22)
    shape = (devices * BLOCKS, 3, PARTICLES)
    jitter = jax.random.uniform(jax.random.fold_in(base, 1), shape, jnp.float32)
    return ((cells[:, :, None] + jitter) * 0.5).astype(jnp.float32)


def draw_send_first(key, part):
    return ghost_tables(key, 11, block_cells(key))[0]


def draw_neighbours_first(key, part):
    return ghost_tables(key, 11, block_cells(key))[1]


def draw_send_second(key, part):
    return ghost_tables(key, 12, moved_cells(key))[0]


def draw_neighbours_second(key, part):
    return ghost_tables(key, 12, moved_cells(key))[1]


def block_scale(key, dims, cuts, least, top_value):
    level = 1.0
    for dim, shards_of in cuts:
        heights = jax.random.uniform(jax.random.fold_in(jax.random.fold_in(key, 6), dim), (shards_of,), jnp.float32, least / len(cuts), top_value / len(cuts))
        level = level * jnp.repeat(jnp.exp(heights), dims[dim] // shards_of).reshape((-1,) + (1,) * (len(dims) - 1 - dim))
    return level


def setup_inputs(seed: int = 0) -> dict:
    splits = jax.random.split(jax.random.key(seed), 9)
    position = draw_position(jax.random.fold_in(splits[8], 71), 0)
    velocity = jnp.clip(jax.random.uniform(splits[1], (ALL_BLOCKS, 3, PARTICLES), jnp.float32, -0.3, 0.3) * block_scale(splits[1], (ALL_BLOCKS, 3, PARTICLES), ((0, 32),), -0.4, 0.0), -0.3, 0.3)
    particle_mass = jnp.clip(jnp.exp(math.log(0.0078125) - 1.3862944 * jax.random.uniform(splits[2], (ALL_BLOCKS, PARTICLES), jnp.float32) ** block_scale(splits[2], (ALL_BLOCKS, PARTICLES), ((0, 32),), -0.2, 0.2)), 0.001953125, 0.0078125)
    send_first = draw_send_first(jax.random.fold_in(splits[8], 71), 0)
    neighbours_first = draw_neighbours_first(jax.random.fold_in(splits[8], 71), 0)
    destination = draw_destination(jax.random.fold_in(splits[8], 71), 0)
    send_second = draw_send_second(jax.random.fold_in(splits[8], 71), 0)
    neighbours_second = draw_neighbours_second(jax.random.fold_in(splits[8], 71), 0)
    return {"position": position, "velocity": velocity, "particle_mass": particle_mass, "send_first": send_first, "neighbours_first": neighbours_first, "destination": destination, "send_second": send_second, "neighbours_second": neighbours_second}


smooth_len = 0.5
time_step = 0.25


def pair_density(home_points, away_points, away_mass):
    offset = home_points[:, :, :, None] - away_points[:, :, None, :]
    squared = jnp.sum(offset * offset, axis=1)
    kernel = jnp.maximum(1.0 - squared / (smooth_len * smooth_len), 0.0)
    return jnp.sum(away_mass[:, None, :] * (kernel * kernel * kernel), axis=2)


def pair_force(home_points, home_term, away_points, away_mass, away_term):
    offset = home_points[:, :, :, None] - away_points[:, :, None, :]
    squared = jnp.sum(offset * offset, axis=1)
    kernel = jnp.maximum(1.0 - squared / (smooth_len * smooth_len), 0.0)
    weight = away_mass[:, None, :] * (home_term[:, :, None] + away_term[:, None, :]) * kernel * kernel
    return (6.0 / (smooth_len * smooth_len)) * jnp.sum(weight[:, None, :, :] * offset, axis=3)


def pressure_term(density):
    return jnp.exp(jnp.log(density) * (-1.0 / 3.0))


def table_density(home_points, home_mass, all_points, all_mass, lookup):
    initial = pair_density(home_points, home_points, home_mass)

    def add_column(column, running):
        picked = lookup[:, column]
        return running + pair_density(home_points, all_points[picked], all_mass[picked])

    return lax.fori_loop(0, lookup.shape[1], add_column, initial)


def table_force(home_points, home_mass, home_term, all_points, all_mass, all_term, lookup):
    initial = pair_force(home_points, home_term, home_points, home_mass, home_term)

    def add_column(column, running):
        picked = lookup[:, column]
        return running + pair_force(home_points, home_term, all_points[picked], all_mass[picked], all_term[picked])

    return lax.fori_loop(0, lookup.shape[1], add_column, initial)


def global_rows(sender, neighbours):
    total_blocks = neighbours.shape[0]
    owner_device = jnp.arange(total_blocks, dtype=jnp.int32) // BLOCKS
    remote = jnp.maximum(neighbours - BLOCKS, 0)
    source = remote // GHOST_CAP
    within = remote % GHOST_CAP
    listed = sender[source, owner_device[:, None], within]
    far_row = jnp.where(listed >= 0, source * BLOCKS + listed, total_blocks)
    return jnp.where(neighbours < BLOCKS, owner_device[:, None] * BLOCKS + neighbours, far_row).astype(jnp.int32)


def sph_forces(points, weights, sender, neighbours):
    total_blocks = points.shape[0]
    groups = total_blocks // BLOCKS
    lookup = global_rows(sender, neighbours)
    all_points = jnp.concatenate([points, jnp.zeros((1,) + points.shape[1:], jnp.float32)], axis=0)
    all_mass = jnp.concatenate([weights, jnp.zeros((1, weights.shape[1]), jnp.float32)], axis=0)
    grouped_points = points.reshape((groups, BLOCKS) + points.shape[1:])
    grouped_mass = weights.reshape(groups, BLOCKS, weights.shape[1])
    grouped_rows = lookup.reshape(groups, BLOCKS, lookup.shape[1])

    def density_group(packed):
        return table_density(packed[0], packed[1], all_points, all_mass, packed[2])

    density = lax.map(density_group, (grouped_points, grouped_mass, grouped_rows)).reshape(weights.shape)
    all_rho = jnp.concatenate([density, jnp.ones((1, density.shape[1]), jnp.float32)], axis=0)
    all_term = pressure_term(all_rho)
    grouped_term = all_term[:total_blocks].reshape(groups, BLOCKS, weights.shape[1])

    def force_group(packed):
        return table_force(packed[0], packed[1], packed[3], all_points, all_mass, all_term, packed[2])

    acceleration = lax.map(force_group, (grouped_points, grouped_mass, grouped_rows, grouped_term)).reshape(points.shape)
    return density, acceleration


def reference(position, velocity, particle_mass, send_first, neighbours_first, destination, send_second, neighbours_second):
    density, acceleration = sph_forces(position, particle_mass, send_first, neighbours_first)
    velocity = velocity + time_step * acceleration
    position = position + time_step * velocity
    position = jnp.zeros_like(position).at[destination].set(position)
    velocity = jnp.zeros_like(velocity).at[destination].set(velocity)
    moved_mass = jnp.zeros_like(particle_mass).at[destination].set(particle_mass)
    density, acceleration = sph_forces(position, moved_mass, send_second, neighbours_second)
    velocity = velocity + time_step * acceleration
    position = position + time_step * velocity
    return position, velocity, density
```

```python
import jax
import jax.numpy as jnp
from jax import lax
from jax.experimental import pallas as pl
from jax.experimental.pallas import tpu as pltpu
from jax.sharding import PartitionSpec as P

AXES = ("gx", "gy", "gz")
MOVE_CAP = 2
SMOOTH_LEN = 0.5
TIME_STEP = 0.25
INVERSE = 1.0 / (SMOOTH_LEN * SMOOTH_LEN)
PART_PAIRS = ((0, 0), (0, 1), (1, 0), (0, 2), (2, 0), (1, 1))
DEPTH = 8 * len(PART_PAIRS)
GROUP = 2
CODES = 27
MESH = pl.DeviceIdType.MESH
VMEM_LIMIT = 40 * 1024 * 1024


def linear(place):
    size_y, size_z = lax.axis_size("gy"), lax.axis_size("gz")
    return (place[0] * size_y + place[1]) * size_z + place[2]


def my_place():
    return tuple(lax.axis_index(axis) for axis in AXES)


def shifted(shift):
    place = tuple(i + s for i, s in zip(my_place(), shift))
    inside = jnp.bool_(True)
    for i, axis in zip(place, AXES):
        inside = inside & (i >= 0) & (i < lax.axis_size(axis))
    return place, inside


def around(code):
    place, inside = shifted((code // 9 - 1, code // 3 % 3 - 1, code % 3 - 1))
    return place, inside & (code != CODES // 2)


def each_neighbour(act):
    def one(code, carry):
        place, inside = around(code)

        @pl.when(inside)
        def _():
            act(place)

        return carry

    lax.fori_loop(0, CODES, one, 0)


def faces():
    found = []
    for axis in range(3):
        for step in (-1, 1):
            found.append(shifted(tuple(step if a == axis else 0 for a in range(3))))
    return found


def greet():
    barrier = pltpu.get_barrier_semaphore()

    def signal(place):
        pl.semaphore_signal(barrier, inc=1, device_id=place, device_id_type=MESH)

    each_neighbour(signal)


def meet():
    count = jnp.int32(1)
    for i, axis in zip(my_place(), AXES):
        size = lax.axis_size(axis)
        count = count * (1 + (i > 0).astype(jnp.int32) + (i < size - 1).astype(jnp.int32))
    pl.semaphore_wait(pltpu.get_barrier_semaphore(), count - 1)


def ghost_copy(send, land, send_sem, recv_sem, place, slot):
    to = linear(place)
    return pltpu.make_async_remote_copy(
        src_ref=send.at[to],
        dst_ref=land.at[slot],
        send_sem=send_sem.at[to],
        recv_sem=recv_sem.at[slot],
        device_id=place,
        device_id_type=MESH,
    )


def swap_start(send, land, send_sem, recv_sem):
    me = linear(my_place())
    each_neighbour(lambda place: ghost_copy(send, land, send_sem, recv_sem, place, me).start())


def swap_wait(send, land, send_sem, recv_sem):
    each_neighbour(
        lambda place: ghost_copy(send, land, send_sem, recv_sem, place, linear(place)).wait()
    )


def points_kernel(rows, points, mass, destination, land, send, send_sem, recv_sem):
    cap = rows.shape[1]
    greet()
    goal = jnp.broadcast_to(destination[...].astype(jnp.float32), (8, destination.shape[1]))

    def fill(place):
        to = linear(place)
        for c in range(cap):
            row = jnp.maximum(rows[to, c], 0)
            send[to, 4 * c : 4 * c + 3] = points[row]
            send[to, 4 * c + 3 : 4 * c + 4] = mass[pl.ds(row, 1), :]
        send[to, 4 * cap : 4 * cap + 8] = goal

    each_neighbour(fill)
    meet()
    swap_start(send, land, send_sem, recv_sem)
    swap_wait(send, land, send_sem, recv_sem)


def density_swap_kernel(rows, density, land, send, send_sem, recv_sem):
    cap = rows.shape[1]
    greet()

    def fill(place):
        to = linear(place)
        for c in range(cap):
            row = jnp.maximum(rows[to, c], 0)
            send[to, c : c + 1] = density[pl.ds(row, 1), :]

    each_neighbour(fill)
    meet()
    swap_start(send, land, send_sem, recv_sem)
    swap_wait(send, land, send_sem, recv_sem)


def move_kernel(
    table, rows, fields, moved, land, outbox, arrived, send, out_sem, in_sem, send_sem, recv_sem
):
    cap = rows.shape[1]
    blocks = fields.shape[0]
    greet()
    for face in range(6):
        for k in range(MOVE_CAP):
            outbox[face, k] = fields[table[8 * (k + 1) + face, 0]]
    meet()

    def block_copy(face, place, slot):
        return pltpu.make_async_remote_copy(
            src_ref=outbox.at[face],
            dst_ref=arrived.at[slot],
            send_sem=out_sem.at[face],
            recv_sem=in_sem.at[slot],
            device_id=place,
            device_id_type=MESH,
        )

    for face, (place, inside) in enumerate(faces()):
        pl.when(inside)(lambda: block_copy(face, place, face ^ 1).start())
    for face, (place, inside) in enumerate(faces()):
        pl.when(inside)(lambda: block_copy(face, place, face).wait())

    def settle(p, carry):
        source = table[0, p]
        kept = fields[jnp.minimum(source, blocks - 1)]
        slot = jnp.maximum(source - blocks, 0)
        came = arrived[slot // MOVE_CAP, slot % MOVE_CAP]
        moved[p] = jnp.where(source < blocks, kept, came)
        return carry

    lax.fori_loop(0, blocks, settle, 0, unroll=8)

    def fill(place):
        to = linear(place)
        for c in range(cap):
            tile = moved[jnp.maximum(rows[to, c], 0)]
            send[to, 4 * c : 4 * c + 3] = tile[0:3]
            send[to, 4 * c + 3 : 4 * c + 4] = tile[6:7]

    each_neighbour(fill)
    swap_start(send, land, send_sem, recv_sem)
    swap_wait(send, land, send_sem, recv_sem)


def pressure_term(density):
    return jnp.exp(jnp.log(density) * (-1.0 / 3.0))


def cube_root(mass):
    return jnp.exp(jnp.log(mass) * (1.0 / 3.0))


def three_parts(value):
    parts = []
    for _ in range(3):
        part = value.astype(jnp.bfloat16).astype(jnp.float32)
        parts.append(part)
        value = value - part
    return parts


def middle(width):
    row = lax.broadcasted_iota(jnp.int32, (3, width), 0)
    place = [i.astype(jnp.float32) + 0.5 for i in my_place()]
    return jnp.where(row == 0, place[0], jnp.where(row == 1, place[1], place[2]))


def far_rows(here, root, square):
    blank = jnp.zeros_like(here)
    far = jnp.concatenate(
        [2.0 * INVERSE * root * here, -INVERSE * root * square, root, blank], axis=0
    )
    parts = three_parts(far)
    return jnp.concatenate([parts[a] for a, _ in PART_PAIRS], axis=0).T.astype(jnp.bfloat16)


def near_rows(here, square):
    near = jnp.concatenate(
        [here, jnp.ones_like(square), 1.0 - INVERSE * square, jnp.zeros_like(here)], axis=0
    )
    parts = three_parts(near)
    return jnp.concatenate([parts[b] for _, b in PART_PAIRS], axis=0).astype(jnp.bfloat16)


def work_out_moves(destination, ghost, table, at):
    blocks = destination.shape[1]
    me = linear(my_place())
    goal = destination[...]
    lane = lax.broadcasted_iota(jnp.int32, (8, blocks), 1)
    face = lax.broadcasted_iota(jnp.int32, (8, blocks), 0)
    theirs, targets = [], []
    for place, inside in faces():
        device = jnp.where(inside, linear(place), -1)
        row = ghost[jnp.maximum(device, 0), at : at + 1].astype(jnp.int32)
        theirs.append(jnp.where(inside, row, -1))
        targets.append(jnp.full((1, blocks), device, jnp.int32))
    theirs += [jnp.full((2, blocks), -1, jnp.int32)]
    targets += [jnp.full((2, blocks), -1, jnp.int32)]
    coming = jnp.concatenate(theirs, axis=0) - me * blocks
    going = goal - jnp.concatenate(targets, axis=0) * blocks

    def picks(offset):
        left = (offset >= 0) & (offset < blocks)
        for k in range(MOVE_CAP):
            first = jnp.min(jnp.where(left, lane, blocks), axis=1, keepdims=True)
            hit = left & (lane == first)
            left = left & (lane != first)
            yield k, first, hit

    source = jnp.zeros((8, blocks), jnp.int32)
    for k, first, hit in picks(coming):
        spot = jnp.sum(jnp.where(hit, coming, 0), axis=1, keepdims=True)
        spot = jnp.where(first < blocks, spot, -1)
        source = source + jnp.where(lane == spot, blocks + face * MOVE_CAP + k, 0)
    source = jnp.sum(source, axis=0, keepdims=True)
    kept = jnp.broadcast_to((goal - me * blocks).astype(jnp.float32), (blocks, blocks)).T
    column = lax.broadcasted_iota(jnp.int32, (blocks, blocks), 1)
    block = lax.broadcasted_iota(jnp.int32, (blocks, blocks), 0)
    stays = jnp.where(kept.astype(jnp.int32) == column, block, 0)
    source = source + jnp.sum(stays, axis=0, keepdims=True)
    table[0:8] = jnp.broadcast_to(source, (8, blocks))
    for k, first, _ in picks(going):
        table[8 * (k + 1) : 8 * (k + 2)] = jnp.broadcast_to(
            jnp.where(first < blocks, first, 0), (8, blocks)
        )


def density_main(lookup, own, ghost, out, home, away):
    blocks, columns = lookup.shape
    width = out.shape[1]
    cap = (away.shape[0] - blocks) // ghost.shape[0]
    centre = middle(width)

    def prepare(r, carry):
        here, mass = own(r)
        here = here - centre
        square = jnp.sum(here * here, axis=0, keepdims=True)
        away[r] = far_rows(here, cube_root(mass), square)
        home[r] = near_rows(here, square)
        return carry

    lax.fori_loop(0, blocks, prepare, 0, unroll=8)

    def prepare_ghosts(place):
        device = linear(place)
        tile = ghost[device]
        for c in range(cap):
            here = tile[4 * c : 4 * c + 3] - centre
            square = jnp.sum(here * here, axis=0, keepdims=True)
            away[blocks + device * cap + c] = far_rows(
                here, cube_root(tile[4 * c + 3 : 4 * c + 4]), square
            )

    each_neighbour(prepare_ghosts)

    def one_block(b):
        rhs = home[b]
        acc = jnp.zeros((8, width), jnp.float32)
        for k in range(columns + 1):
            row = b if k == 0 else lookup[b, k - 1]
            w = jnp.dot(away[row], rhs, preferred_element_type=jnp.float32)
            w = jnp.maximum(w, 0.0)
            w = w * w * w
            acc = acc + jnp.sum(w.reshape(w.shape[0] // 8, 8, width), axis=0)
        out[pl.ds(b, 1), :] = jnp.sum(acc, axis=0, keepdims=True)

    several(blocks, 8, one_block)


def several(count, most, act):
    size = most
    while count % size:
        size //= 2

    def step(s, carry):
        for u in range(size):
            act(s * size + u)
        return carry

    lax.fori_loop(0, count // size, step, 0)


def force_main(lookup, home, away, own, ghost, density, ghost_density, finish, moment, term):
    blocks, columns = lookup.shape
    width = density.shape[1]
    cap = ghost_density.shape[1]
    centre = middle(width)
    term[...] = pressure_term(density[...])

    def moments(here, mass, q):
        root = cube_root(mass)
        plain = jnp.concatenate([root, root * here], axis=0)
        full = jnp.concatenate([plain, plain * q], axis=0)
        high = full.astype(jnp.bfloat16).astype(jnp.float32)
        return jnp.concatenate([high, full - high], axis=0).astype(jnp.bfloat16)

    def prepare(r, carry):
        here, mass = own(r)
        moment[r] = moments(here - centre, mass, term[pl.ds(r, 1), :])
        return carry

    lax.fori_loop(0, blocks, prepare, 0, unroll=8)

    def prepare_ghosts(place):
        device = linear(place)
        tile = ghost[device]
        q = pressure_term(ghost_density[device])
        for c in range(cap):
            here = tile[4 * c : 4 * c + 3] - centre
            moment[blocks + device * cap + c] = moments(
                here, tile[4 * c + 3 : 4 * c + 4], q[c : c + 1]
            )

    each_neighbour(prepare_ghosts)

    def one_block(b):
        rhs = home[b]
        acc = jnp.zeros((16, 2 * width), jnp.float32)
        rows = [b] + [lookup[b, k] for k in range(columns)]
        for start in range(0, columns + 1, GROUP):
            group = rows[start : start + GROUP]
            parts = []
            for row in group:
                w = jnp.dot(away[row], rhs, preferred_element_type=jnp.float32)
                w = jnp.maximum(w, 0.0)
                w = w * w
                high = w.astype(jnp.bfloat16)
                low = (w - high.astype(jnp.float32)).astype(jnp.bfloat16)
                parts.append(jnp.concatenate([high, low], axis=1))
            feature = jnp.concatenate([moment[row] for row in group], axis=1)
            both = jnp.concatenate(parts, axis=0)
            acc = acc + jnp.dot(feature, both, preferred_element_type=jnp.float32)
        acc = acc[:, :width] + acc[:, width:]
        sums = acc[0:8] + acc[8:16]
        q = term[pl.ds(b, 1), :]
        here = own(b)[0] - centre
        near = here * sums[0:1] - sums[1:4]
        far = here * sums[4:5] - sums[5:8]
        finish(b, 6.0 * INVERSE * (q * near + far))

    several(blocks, 4, one_block)


def own_of_arrays(points, mass):
    return lambda r: (points[r], mass[pl.ds(r, 1), :])


def own_of_fields(fields):
    def own(r):
        tile = fields[r]
        return tile[0:3], tile[6:7]

    return own


def first_density_kernel(lookup, points, mass, ghost, destination, out, home, away, table):
    cap = (away.shape[0] - lookup.shape[0]) // ghost.shape[0]
    work_out_moves(destination, ghost, table, 4 * cap)
    density_main(lookup, own_of_arrays(points, mass), ghost, out, home, away)


def second_density_kernel(lookup, fields, ghost, out, home, away):
    density_main(lookup, own_of_fields(fields), ghost, out, home, away)


def first_force_kernel(
    lookup, home, away, points, velocity, mass, ghost, density, ghost_density, fields, moment, term
):
    def finish(b, acceleration):
        speed = velocity[b] + TIME_STEP * acceleration
        place = points[b] + TIME_STEP * speed
        weight = mass[pl.ds(b, 1), :]
        fields[b] = jnp.concatenate([place, speed, weight, weight], axis=0)

    own = own_of_arrays(points, mass)
    force_main(lookup, home, away, own, ghost, density, ghost_density, finish, moment, term)


def second_force_kernel(
    lookup, home, away, fields, ghost, density, ghost_density, points_out, speed_out, moment, term
):
    def finish(b, acceleration):
        tile = fields[b]
        speed = tile[3:6] + TIME_STEP * acceleration
        speed_out[b] = speed
        points_out[b] = tile[0:3] + TIME_STEP * speed

    own = own_of_fields(fields)
    force_main(lookup, home, away, own, ghost, density, ghost_density, finish, moment, term)


def call(body, scalars, operands, outs, scratch=(), collective_id=None):
    vmem = pl.BlockSpec(memory_space=pltpu.VMEM)
    smem = pl.BlockSpec(memory_space=pltpu.SMEM)
    return pl.pallas_call(
        body,
        out_shape=[jax.ShapeDtypeStruct(shape, dtype) for shape, dtype in outs],
        in_specs=[smem] * len(scalars) + [vmem] * len(operands),
        out_specs=[vmem] * len(outs),
        scratch_shapes=scratch,
        compiler_params=pltpu.CompilerParams(
            vmem_limit_bytes=VMEM_LIMIT,
            collective_id=collective_id,
            has_side_effects=collective_id is not None,
        ),
    )(*scalars, *operands)


def per_device(
    position,
    velocity,
    particle_mass,
    send_first,
    neighbours_first,
    destination,
    send_second,
    neighbours_second,
):
    blocks, _, width = position.shape
    _, devices, cap = send_first.shape
    total = blocks + devices * cap
    single, half = jnp.float32, jnp.bfloat16
    pair = [pltpu.SemaphoreType.DMA((devices,))] * 2
    features = [((blocks, DEPTH, width), half), ((total, width, DEPTH), half)]
    force_scratch = [pltpu.VMEM((total, 16, width), half), pltpu.VMEM((blocks, width), single)]
    destination = destination.reshape(1, blocks)

    def swap_density(rows, density, collective_id):
        return call(
            density_swap_kernel,
            [rows],
            [density],
            [((devices, cap, width), single)],
            [pltpu.VMEM((devices, cap, width), single), *pair],
            collective_id,
        )[0]

    with_goal = (devices, 4 * cap + 8, width)
    (ghost,) = call(
        points_kernel,
        [send_first[0]],
        [position, particle_mass, destination],
        [(with_goal, single)],
        [pltpu.VMEM(with_goal, single), *pair],
        0,
    )
    density, home, away, table = call(
        first_density_kernel,
        [neighbours_first],
        [position, particle_mass, ghost, destination],
        [((blocks, width), single), *features, ((8 * (MOVE_CAP + 1), blocks), jnp.int32)],
    )
    ghost_density = swap_density(send_first[0], density, 1)
    (fields,) = call(
        first_force_kernel,
        [neighbours_first],
        [home, away, position, velocity, particle_mass, ghost, density, ghost_density],
        [((blocks, 8, width), single)],
        force_scratch,
    )
    box = (6, MOVE_CAP, 8, width)
    fields, ghost = call(
        move_kernel,
        [table, send_second[0]],
        [fields],
        [((blocks, 8, width), single), ((devices, 4 * cap, width), single)],
        [
            pltpu.VMEM(box, single),
            pltpu.VMEM(box, single),
            pltpu.VMEM((devices, 4 * cap, width), single),
            pltpu.SemaphoreType.DMA((6,)),
            pltpu.SemaphoreType.DMA((6,)),
            *pair,
        ],
        2,
    )
    density, home, away = call(
        second_density_kernel,
        [neighbours_second],
        [fields, ghost],
        [((blocks, width), single), *features],
    )
    ghost_density = swap_density(send_second[0], density, 3)
    position, velocity = call(
        second_force_kernel,
        [neighbours_second],
        [home, away, fields, ghost, density, ghost_density],
        [((blocks, 3, width), single)] * 2,
        force_scratch,
    )
    return position, velocity, density


def solution(mesh):
    whole, flat = P(AXES, None, None), P(AXES, None)
    return jax.shard_map(
        per_device,
        mesh=mesh,
        in_specs=(whole, whole, flat, whole, flat, P(AXES), whole, flat),
        out_specs=(whole, whole, flat),
        check_vma=False,
    )
```

```python
import jax
import jax.numpy as jnp
from jax import lax
from jax.experimental import pallas as pl
from jax.experimental.pallas import tpu as pltpu
from jax.sharding import PartitionSpec as P

AXES = ("gx", "gy", "gz")
MOVE_CAP = 2
SMOOTH_LEN = 0.5
TIME_STEP = 0.25
INVERSE = 1.0 / (SMOOTH_LEN * SMOOTH_LEN)
PART_PAIRS = ((0, 0), (0, 1), (1, 0), (0, 2), (2, 0), (1, 1))
DEPTH = 8 * len(PART_PAIRS)
GROUP = 1
CODES = 27
MESH = pl.DeviceIdType.MESH
VMEM_LIMIT = 40 * 1024 * 1024


def linear(place):
    size_y, size_z = lax.axis_size("gy"), lax.axis_size("gz")
    return (place[0] * size_y + place[1]) * size_z + place[2]


def my_place():
    return tuple(lax.axis_index(axis) for axis in AXES)


def shifted(shift):
    place = tuple(i + s for i, s in zip(my_place(), shift))
    inside = jnp.bool_(True)
    for i, axis in zip(place, AXES):
        inside = inside & (i >= 0) & (i < lax.axis_size(axis))
    return place, inside


def around(code):
    place, inside = shifted((code // 9 - 1, code // 3 % 3 - 1, code % 3 - 1))
    return place, inside & (code != CODES // 2)


def each_neighbour(act):
    def one(code, carry):
        place, inside = around(code)

        @pl.when(inside)
        def _():
            act(place)

        return carry

    lax.fori_loop(0, CODES, one, 0)


def faces():
    found = []
    for axis in range(3):
        for step in (-1, 1):
            found.append(shifted(tuple(step if a == axis else 0 for a in range(3))))
    return found


def greet():
    barrier = pltpu.get_barrier_semaphore()

    def signal(place):
        pl.semaphore_signal(barrier, inc=1, device_id=place, device_id_type=MESH)

    each_neighbour(signal)


def meet():
    count = jnp.int32(1)
    for i, axis in zip(my_place(), AXES):
        size = lax.axis_size(axis)
        count = count * (1 + (i > 0).astype(jnp.int32) + (i < size - 1).astype(jnp.int32))
    pl.semaphore_wait(pltpu.get_barrier_semaphore(), count - 1)


def ghost_copy(send, land, send_sem, recv_sem, place, slot):
    to = linear(place)
    return pltpu.make_async_remote_copy(
        src_ref=send.at[to],
        dst_ref=land.at[slot],
        send_sem=send_sem.at[to],
        recv_sem=recv_sem.at[slot],
        device_id=place,
        device_id_type=MESH,
    )


def swap_start(send, land, send_sem, recv_sem):
    me = linear(my_place())
    each_neighbour(lambda place: ghost_copy(send, land, send_sem, recv_sem, place, me).start())


def swap_wait(send, land, send_sem, recv_sem):
    each_neighbour(
        lambda place: ghost_copy(send, land, send_sem, recv_sem, place, linear(place)).wait()
    )


def fill_points(rows, tiles, extra, send):
    cap = rows.shape[0]

    def fill(place):
        to = linear(place)
        for c in range(cap):
            send[to, 4 * c : 4 * c + 4] = tiles[jnp.maximum(rows[c, to], 0)][0:4]
        if extra is not None:
            send[to, 4 * cap : 4 * cap + 8] = extra

    each_neighbour(fill)


def send_density(rows, density, land, send, sems):
    cap = rows.shape[0]

    def fill(place):
        to = linear(place)
        for c in range(cap):
            row = jnp.maximum(rows[c, to], 0)
            send[to, c : c + 1] = density[pl.ds(row, 1), :]

    each_neighbour(fill)
    swap_start(send, land, *sems)
    swap_wait(send, land, *sems)


def move_blocks(table, tiles, moved, outbox, arrived, out_sem, in_sem):
    blocks = tiles.shape[0]

    def block_copy(face, place, slot):
        return pltpu.make_async_remote_copy(
            src_ref=outbox.at[face],
            dst_ref=arrived.at[slot],
            send_sem=out_sem.at[face],
            recv_sem=in_sem.at[slot],
            device_id=place,
            device_id_type=MESH,
        )

    for face, (place, inside) in enumerate(faces()):
        pl.when(inside)(lambda: block_copy(face, place, face ^ 1).start())
    for face, (place, inside) in enumerate(faces()):
        pl.when(inside)(lambda: block_copy(face, place, face).wait())

    def settle(p, carry):
        source = table[0, p]
        kept = tiles[jnp.minimum(source, blocks - 1)]
        slot = jnp.maximum(source - blocks, 0)
        came = arrived[slot // MOVE_CAP, slot % MOVE_CAP]
        moved[p] = jnp.where(source < blocks, kept, came)
        return carry

    lax.fori_loop(0, blocks, settle, 0, unroll=8)


def pressure_term(density):
    return jnp.exp(jnp.log(density) * (-1.0 / 3.0))


def cube_root(mass):
    return jnp.exp(jnp.log(mass) * (1.0 / 3.0))


def three_parts(value):
    parts = []
    for _ in range(3):
        part = value.astype(jnp.bfloat16).astype(jnp.float32)
        parts.append(part)
        value = value - part
    return parts


def middle(width):
    row = lax.broadcasted_iota(jnp.int32, (3, width), 0)
    place = [i.astype(jnp.float32) + 0.5 for i in my_place()]
    return jnp.where(row == 0, place[0], jnp.where(row == 1, place[1], place[2]))


def far_rows(here, root, square):
    blank = jnp.zeros_like(here)
    far = jnp.concatenate(
        [2.0 * INVERSE * root * here, -INVERSE * root * square, root, blank], axis=0
    )
    parts = three_parts(far)
    return jnp.concatenate([parts[a] for a, _ in PART_PAIRS], axis=0).T.astype(jnp.bfloat16)


def near_rows(here, square):
    near = jnp.concatenate(
        [here, jnp.ones_like(square), 1.0 - INVERSE * square, jnp.zeros_like(here)], axis=0
    )
    parts = three_parts(near)
    return jnp.concatenate([parts[b] for _, b in PART_PAIRS], axis=0).astype(jnp.bfloat16)


def work_out_moves(destination, ghost, table, at):
    blocks = destination.shape[1]
    me = linear(my_place())
    goal = destination[...]
    lane = lax.broadcasted_iota(jnp.int32, (8, blocks), 1)
    face = lax.broadcasted_iota(jnp.int32, (8, blocks), 0)
    theirs, targets = [], []
    for place, inside in faces():
        device = jnp.where(inside, linear(place), -1)
        row = ghost[jnp.maximum(device, 0), at : at + 1].astype(jnp.int32)
        theirs.append(jnp.where(inside, row, -1))
        targets.append(jnp.full((1, blocks), device, jnp.int32))
    theirs += [jnp.full((2, blocks), -1, jnp.int32)]
    targets += [jnp.full((2, blocks), -1, jnp.int32)]
    coming = jnp.concatenate(theirs, axis=0) - me * blocks
    going = goal - jnp.concatenate(targets, axis=0) * blocks

    def picks(offset):
        left = (offset >= 0) & (offset < blocks)
        for k in range(MOVE_CAP):
            first = jnp.min(jnp.where(left, lane, blocks), axis=1, keepdims=True)
            hit = left & (lane == first)
            left = left & (lane != first)
            yield k, first, hit

    source = jnp.zeros((8, blocks), jnp.int32)
    for k, first, hit in picks(coming):
        spot = jnp.sum(jnp.where(hit, coming, 0), axis=1, keepdims=True)
        spot = jnp.where(first < blocks, spot, -1)
        source = source + jnp.where(lane == spot, blocks + face * MOVE_CAP + k, 0)
    source = jnp.sum(source, axis=0, keepdims=True)
    kept = jnp.broadcast_to((goal - me * blocks).astype(jnp.float32), (blocks, blocks)).T
    column = lax.broadcasted_iota(jnp.int32, (blocks, blocks), 1)
    block = lax.broadcasted_iota(jnp.int32, (blocks, blocks), 0)
    stays = jnp.where(kept.astype(jnp.int32) == column, block, 0)
    source = source + jnp.sum(stays, axis=0, keepdims=True)
    table[0:8] = jnp.broadcast_to(source, (8, blocks))
    for k, first, _ in picks(going):
        table[8 * (k + 1) : 8 * (k + 2)] = jnp.broadcast_to(
            jnp.where(first < blocks, first, 0), (8, blocks)
        )


def prepare_own(tiles, home, away):
    centre = middle(tiles.shape[2])

    def prepare(r, carry):
        tile = tiles[r]
        here = tile[0:3] - centre
        square = jnp.sum(here * here, axis=0, keepdims=True)
        away[r] = far_rows(here, cube_root(tile[3:4]), square)
        home[r] = near_rows(here, square)
        return carry

    lax.fori_loop(0, tiles.shape[0], prepare, 0, unroll=8)


def prepare_ghosts(blocks, cap, ghost, away):
    centre = middle(ghost.shape[2])

    def prepare(place):
        device = linear(place)
        for c in range(cap):
            tile = ghost[device, 4 * c : 4 * c + 4]
            here = tile[0:3] - centre
            square = jnp.sum(here * here, axis=0, keepdims=True)
            away[blocks + device * cap + c] = far_rows(here, cube_root(tile[3:4]), square)

    each_neighbour(prepare)


def sum_densities(lookup, home, away, out):
    columns, blocks = lookup.shape
    width = out.shape[1]

    def one_block(b):
        rhs = home[b]
        acc = jnp.zeros((8, width), jnp.float32)
        for k in range(columns + 1):
            row = b if k == 0 else lookup[k - 1, b]
            w = jnp.dot(away[row], rhs, preferred_element_type=jnp.float32)
            w = jnp.maximum(w, 0.0)
            w = w * w * w
            acc = acc + jnp.sum(w.reshape(w.shape[0] // 8, 8, width), axis=0)
        out[pl.ds(b, 1), :] = jnp.sum(acc, axis=0, keepdims=True)

    several(blocks, 8, one_block)


def several(count, most, act):
    size = most
    while count % size:
        size //= 2

    def step(s, carry):
        for u in range(size):
            act(s * size + u)
        return carry

    lax.fori_loop(0, count // size, step, 0)


def sum_forces(lookup, home, away, tiles, ghost, density, ghost_density, finish, moment, term):
    columns, blocks = lookup.shape
    width = density.shape[1]
    cap = ghost_density.shape[1]
    centre = middle(width)
    term[...] = pressure_term(density[...])

    def moments(tile, q):
        root = cube_root(tile[3:4])
        plain = jnp.concatenate([root, root * (tile[0:3] - centre)], axis=0)
        full = jnp.concatenate([plain, plain * q], axis=0)
        high = full.astype(jnp.bfloat16).astype(jnp.float32)
        return jnp.concatenate([high, full - high], axis=0).astype(jnp.bfloat16)

    def prepare(r, carry):
        moment[r] = moments(tiles[r], term[pl.ds(r, 1), :])
        return carry

    lax.fori_loop(0, blocks, prepare, 0, unroll=8)

    def prepare_ghosts(place):
        device = linear(place)
        q = pressure_term(ghost_density[device])
        for c in range(cap):
            moment[blocks + device * cap + c] = moments(
                ghost[device, 4 * c : 4 * c + 4], q[c : c + 1]
            )

    each_neighbour(prepare_ghosts)

    def one_block(b):
        rhs = home[b]
        acc = jnp.zeros((16, 2 * width), jnp.float32)
        rows = [b] + [lookup[k, b] for k in range(columns)]
        for start in range(0, columns + 1, GROUP):
            group = rows[start : start + GROUP]
            parts = []
            for row in group:
                w = jnp.dot(away[row], rhs, preferred_element_type=jnp.float32)
                w = jnp.maximum(w, 0.0)
                w = w * w
                high = w.astype(jnp.bfloat16)
                low = (w - high.astype(jnp.float32)).astype(jnp.bfloat16)
                parts.append(jnp.concatenate([high, low], axis=1))
            feature = jnp.concatenate([moment[row] for row in group], axis=1)
            both = jnp.concatenate(parts, axis=0)
            acc = acc + jnp.dot(feature, both, preferred_element_type=jnp.float32)
        acc = acc[:, :width] + acc[:, width:]
        sums = acc[0:8] + acc[8:16]
        q = term[pl.ds(b, 1), :]
        tile = tiles[b]
        here = tile[0:3] - centre
        near = here * sums[0:1] - sums[1:4]
        far = here * sums[4:5] - sums[5:8]
        finish(b, tile, 6.0 * INVERSE * (q * near + far))

    several(blocks, 8, one_block)


def first_stage_kernel(
    rows,
    lookup,
    points,
    velocity,
    mass,
    destination,
    tiles,
    ghost,
    density,
    ghost_density,
    home,
    away,
    table,
    send,
    thin_send,
    *scratch,
):
    *here, fetch_sem, s0, s1, s2, s3 = scratch
    sems = (s0, s1, s2, s3)
    far = (points, velocity, mass, destination, lookup)
    fetches = [
        pltpu.make_async_copy(far[n], here[n], fetch_sem.at[n]) for n in range(len(far))
    ]
    for fetch in fetches:
        fetch.start()
    points, velocity, mass, destination, lookup = here
    cap, _ = rows.shape
    blocks = mass.shape[0]
    greet()
    for fetch in fetches:
        fetch.wait()

    def gather(r, carry):
        row = pl.ds(r, 1)
        for c in range(3):
            tiles[r, c : c + 1] = points[c, row, :]
            tiles[r, c + 4 : c + 5] = velocity[c, row, :]
        tiles[r, 3:4] = mass[row, :]
        tiles[r, 7:8] = mass[row, :]
        return carry

    lax.fori_loop(0, blocks, gather, 0, unroll=8)
    goal = jnp.broadcast_to(destination[...].astype(jnp.float32), (8, blocks))
    fill_points(rows, tiles, goal, send)
    meet()
    swap_start(send, ghost, *sems[0:2])
    prepare_own(tiles, home, away)
    swap_wait(send, ghost, *sems[0:2])
    work_out_moves(destination, ghost, table, 4 * cap)
    prepare_ghosts(blocks, cap, ghost, away)
    sum_densities(lookup, home, away, density)
    send_density(rows, density, ghost_density, thin_send, sems[2:4])


def second_stage_kernel(
    table,
    rows,
    lookup,
    tiles,
    moved,
    ghost,
    density,
    ghost_density,
    home,
    away,
    send,
    thin_send,
    outbox,
    arrived,
    *sems,
):
    cap, _ = rows.shape
    blocks = tiles.shape[0]
    greet()
    for face in range(6):
        for k in range(MOVE_CAP):
            outbox[face, k] = tiles[table[8 * (k + 1) + face, 0]]
    meet()
    move_blocks(table, tiles, moved, outbox, arrived, *sems[4:6])
    fill_points(rows, moved, None, send)
    swap_start(send, ghost, *sems[0:2])
    prepare_own(moved, home, away)
    swap_wait(send, ghost, *sems[0:2])
    prepare_ghosts(blocks, cap, ghost, away)
    sum_densities(lookup, home, away, density)
    send_density(rows, density, ghost_density, thin_send, sems[2:4])


def first_force_kernel(
    lookup, home, away, tiles, ghost, density, ghost_density, new_tiles, moment, term
):
    def finish(b, tile, acceleration):
        speed = tile[4:7] + TIME_STEP * acceleration
        place = tile[0:3] + TIME_STEP * speed
        new_tiles[b] = jnp.concatenate([place, tile[3:4], speed, tile[3:4]], axis=0)

    sum_forces(lookup, home, away, tiles, ghost, density, ghost_density, finish, moment, term)


def second_force_kernel(
    lookup, home, away, tiles, ghost, density, ghost_density, points_out, speed_out, moment, term
):
    def finish(b, tile, acceleration):
        speed = tile[4:7] + TIME_STEP * acceleration
        place = tile[0:3] + TIME_STEP * speed
        for c in range(3):
            speed_out[c, pl.ds(b, 1), :] = speed[c : c + 1]
            points_out[c, pl.ds(b, 1), :] = place[c : c + 1]

    sum_forces(lookup, home, away, tiles, ghost, density, ghost_density, finish, moment, term)


def call(body, scalars, operands, outs, scratch=(), collective_id=None, distant=()):
    vmem = pl.BlockSpec(memory_space=pltpu.VMEM)
    smem = pl.BlockSpec(memory_space=pltpu.SMEM)
    hbm = pl.BlockSpec(memory_space=pltpu.HBM)
    return pl.pallas_call(
        body,
        out_shape=[jax.ShapeDtypeStruct(shape, dtype) for shape, dtype in outs],
        in_specs=[smem] * len(scalars) + [hbm] * len(distant) + [vmem] * len(operands),
        out_specs=[vmem] * len(outs),
        scratch_shapes=scratch,
        compiler_params=pltpu.CompilerParams(
            vmem_limit_bytes=VMEM_LIMIT,
            collective_id=collective_id,
            has_side_effects=collective_id is not None,
        ),
    )(*scalars, *[pltpu.with_memory_space_constraint(a, pltpu.HBM) for a in distant], *operands)


def per_device(
    position,
    velocity,
    particle_mass,
    send_first,
    neighbours_first,
    destination,
    send_second,
    neighbours_second,
):
    blocks, _, width = position.shape
    _, devices, cap = send_first.shape
    total = blocks + devices * cap
    single, half = jnp.float32, jnp.bfloat16
    turn = lambda a: jnp.transpose(a, (1, 0, 2))
    rows_first, rows_second = send_first[0].T, send_second[0].T
    lookup_first, lookup_second = neighbours_first.T, neighbours_second.T
    sems = [pltpu.SemaphoreType.DMA((devices,))] * 4
    tile_shape = ((blocks, 8, width), single)
    thin = (devices, cap, width)
    box = (6, MOVE_CAP, 8, width)
    results = [
        ((blocks, width), single),
        (thin, single),
        ((blocks, DEPTH, width), half),
        ((total, width, DEPTH), half),
    ]
    force_scratch = [pltpu.VMEM((total, 16, width), half), pltpu.VMEM((blocks, width), single)]

    wide = (devices, 4 * cap + 8, width)
    given = [turn(position), turn(velocity), particle_mass, destination.reshape(1, blocks)]
    tiles, ghost, density, ghost_density, home, away, table = call(
        first_stage_kernel,
        [rows_first],
        [],
        [tile_shape, (wide, single), *results, ((8 * (MOVE_CAP + 1), blocks), jnp.int32)],
        [
            pltpu.VMEM(wide, single),
            pltpu.VMEM(thin, single),
            *[pltpu.VMEM(a.shape, a.dtype) for a in given],
            pltpu.SMEM(lookup_first.shape, jnp.int32),
            pltpu.SemaphoreType.DMA((len(given) + 1,)),
            *sems,
        ],
        0,
        [lookup_first, *given],
    )
    (tiles,) = call(
        first_force_kernel,
        [lookup_first],
        [home, away, tiles, ghost, density, ghost_density],
        [tile_shape],
        force_scratch,
    )
    wide = (devices, 4 * cap, width)
    tiles, ghost, density, ghost_density, home, away = call(
        second_stage_kernel,
        [table, rows_second, lookup_second],
        [tiles],
        [tile_shape, (wide, single), *results],
        [
            pltpu.VMEM(wide, single),
            pltpu.VMEM(thin, single),
            pltpu.VMEM(box, single),
            pltpu.VMEM(box, single),
            *sems,
            *[pltpu.SemaphoreType.DMA((6,))] * 2,
        ],
        1,
    )
    position, velocity = call(
        second_force_kernel,
        [lookup_second],
        [home, away, tiles, ghost, density, ghost_density],
        [((3, blocks, width), single)] * 2,
        force_scratch,
    )
    return turn(position), turn(velocity), density


def solution(mesh):
    whole, flat = P(AXES, None, None), P(AXES, None)
    return jax.shard_map(
        per_device,
        mesh=mesh,
        in_specs=(whole, whole, flat, whole, flat, P(AXES), whole, flat),
        out_specs=(whole, whole, flat),
        check_vma=False,
    )
```

```python
import jax
import jax.numpy as jnp
from jax import lax
from jax.experimental import pallas as pl
from jax.experimental.pallas import tpu as pltpu
from jax.sharding import PartitionSpec as P

AXES = ("gx", "gy", "gz")
MOVE_CAP = 2
SMOOTH_LEN = 0.5
TIME_STEP = 0.25
INVERSE = 1.0 / (SMOOTH_LEN * SMOOTH_LEN)
PART_PAIRS = ((0, 0), (0, 1), (1, 0), (0, 2), (2, 0), (1, 1))
DEPTH = 8 * len(PART_PAIRS)
MESH = pl.DeviceIdType.MESH
UNROLL = 8
VMEM_LIMIT = 60 * 1024 * 1024
VMEM_PLAN = 57 * 1024 * 1024


def linear(place):
    size_y, size_z = lax.axis_size("gy"), lax.axis_size("gz")
    return (place[0] * size_y + place[1]) * size_z + place[2]


def my_place():
    return tuple(lax.axis_index(axis) for axis in AXES)


def shifted(shift):
    place = tuple(i + s for i, s in zip(my_place(), shift))
    inside = jnp.bool_(True)
    for i, axis in zip(place, AXES):
        inside = inside & (i >= 0) & (i < lax.axis_size(axis))
    return place, inside


def span(axis):
    i = lax.axis_index(axis)
    return jnp.maximum(i - 1, 0), jnp.minimum(i + 2, lax.axis_size(axis))


def each_place(act):
    (x_low, x_high), (y_low, y_high), (z_low, z_high) = (span(axis) for axis in AXES)
    size_z = lax.axis_size("gz")

    def along_y(y, x):
        act([(x, y, z_low + n) for n in range(min(size_z, 2))])
        if size_z > 2:
            pl.when(z_low + 2 < z_high)(lambda: act([(x, y, z_low + 2)]))
        return x

    def along_x(x, carry):
        lax.fori_loop(y_low, y_high, along_y, x)
        return carry

    lax.fori_loop(x_low, x_high, along_x, 0)


def each_neighbour(act):
    me = linear(my_place())

    def column(places):
        for place in places:
            pl.when(linear(place) != me)(lambda place=place: act(place))

    each_place(column)


def faces():
    found = []
    for axis in range(3):
        for step in (-1, 1):
            found.append(shifted(tuple(step if a == axis else 0 for a in range(3))))
    return found


def greet():
    barrier = pltpu.get_barrier_semaphore()

    def signal(place):
        pl.semaphore_signal(barrier, inc=1, device_id=place, device_id_type=MESH)

    each_neighbour(signal)


def meet():
    count = jnp.int32(1)
    for i, axis in zip(my_place(), AXES):
        size = lax.axis_size(axis)
        count = count * (1 + (i > 0).astype(jnp.int32) + (i < size - 1).astype(jnp.int32))
    pl.semaphore_wait(pltpu.get_barrier_semaphore(), count - 1)


def ghost_copy(send, land, send_sem, recv_sem, place, slot):
    to = linear(place)
    return pltpu.make_async_remote_copy(
        src_ref=send.at[to],
        dst_ref=land.at[slot],
        send_sem=send_sem.at[to],
        recv_sem=recv_sem.at[slot],
        device_id=place,
        device_id_type=MESH,
    )


def swap_start(send, land, send_sem, recv_sem):
    me = linear(my_place())
    each_neighbour(lambda place: ghost_copy(send, land, send_sem, recv_sem, place, me).start())


def swap_wait(send, land, send_sem, recv_sem):
    each_neighbour(
        lambda place: ghost_copy(send, land, send_sem, recv_sem, place, linear(place)).wait()
    )


def fill_points(rows, tiles, extra, send):
    cap = rows.shape[0]

    def fill(place):
        to = linear(place)
        for c in range(cap):
            send[to, 4 * c : 4 * c + 4] = tiles[jnp.maximum(rows[c, to], 0)][0:4]
        if extra is not None:
            send[to, 4 * cap : 4 * cap + 8] = extra

    each_neighbour(fill)


def fill_density(rows, density, send):
    def fill(place):
        to = linear(place)
        for c in range(rows.shape[0]):
            row = jnp.maximum(rows[c, to], 0)
            send[to, c : c + 1] = density[pl.ds(row, 1), :]

    each_neighbour(fill)


def move_blocks(table, tiles, moved, outbox, arrived, out_sem, in_sem):
    blocks = tiles.shape[0]

    def block_copy(face, place, slot):
        return pltpu.make_async_remote_copy(
            src_ref=outbox.at[face],
            dst_ref=arrived.at[slot],
            send_sem=out_sem.at[face],
            recv_sem=in_sem.at[slot],
            device_id=place,
            device_id_type=MESH,
        )

    for face, (place, inside) in enumerate(faces()):
        pl.when(inside)(lambda: block_copy(face, place, face ^ 1).start())
    for face, (place, inside) in enumerate(faces()):
        pl.when(inside)(lambda: block_copy(face, place, face).wait())

    def settle(p, carry):
        source = table[0, p]
        kept = tiles[jnp.minimum(source, blocks - 1)]
        slot = jnp.maximum(source - blocks, 0)
        came = arrived[slot // MOVE_CAP, slot % MOVE_CAP]
        moved[p] = jnp.where(source < blocks, kept, came)
        return carry

    lax.fori_loop(0, blocks, settle, 0, unroll=8)


def pressure_term(density):
    return jnp.exp(jnp.log(density) * (-1.0 / 3.0))


def cube_root(mass):
    return jnp.exp(jnp.log(mass) * (1.0 / 3.0))


def three_parts(value):
    parts = []
    for _ in range(3):
        part = value.astype(jnp.bfloat16).astype(jnp.float32)
        parts.append(part)
        value = value - part
    return parts


def middle(width):
    row = lax.broadcasted_iota(jnp.int32, (3, width), 0)
    place = [i.astype(jnp.float32) + 0.5 for i in my_place()]
    return jnp.where(row == 0, place[0], jnp.where(row == 1, place[1], place[2]))


def far_rows(here, root, square):
    blank = jnp.zeros_like(here)
    far = jnp.concatenate(
        [2.0 * INVERSE * root * here, -INVERSE * root * square, root, blank], axis=0
    )
    parts = three_parts(far)
    return jnp.concatenate([parts[a] for a, _ in PART_PAIRS], axis=0).T.astype(jnp.bfloat16)


def near_rows(here, square):
    near = jnp.concatenate(
        [here, jnp.ones_like(square), 1.0 - INVERSE * square, jnp.zeros_like(here)], axis=0
    )
    parts = three_parts(near)
    return jnp.concatenate([parts[b] for _, b in PART_PAIRS], axis=0).astype(jnp.bfloat16)


def work_out_moves(destination, ghost, table, at):
    blocks = destination.shape[1]
    me = linear(my_place())
    goal = destination[...]
    lane = lax.broadcasted_iota(jnp.int32, (8, blocks), 1)
    face = lax.broadcasted_iota(jnp.int32, (8, blocks), 0)
    theirs, targets = [], []
    for place, inside in faces():
        device = jnp.where(inside, linear(place), -1)
        row = ghost[jnp.maximum(device, 0), at : at + 1].astype(jnp.int32)
        theirs.append(jnp.where(inside, row, -1))
        targets.append(jnp.full((1, blocks), device, jnp.int32))
    theirs += [jnp.full((2, blocks), -1, jnp.int32)]
    targets += [jnp.full((2, blocks), -1, jnp.int32)]
    coming = jnp.concatenate(theirs, axis=0) - me * blocks
    going = goal - jnp.concatenate(targets, axis=0) * blocks

    def picks(offset):
        left = (offset >= 0) & (offset < blocks)
        for k in range(MOVE_CAP):
            first = jnp.min(jnp.where(left, lane, blocks), axis=1, keepdims=True)
            hit = left & (lane == first)
            left = left & (lane != first)
            yield k, first, hit

    source = jnp.zeros((8, blocks), jnp.int32)
    for k, first, hit in picks(coming):
        spot = jnp.sum(jnp.where(hit, coming, 0), axis=1, keepdims=True)
        spot = jnp.where(first < blocks, spot, -1)
        source = source + jnp.where(lane == spot, blocks + face * MOVE_CAP + k, 0)
    source = jnp.sum(source, axis=0, keepdims=True)
    kept = jnp.broadcast_to((goal - me * blocks).astype(jnp.float32), (blocks, blocks)).T
    column = lax.broadcasted_iota(jnp.int32, (blocks, blocks), 1)
    block = lax.broadcasted_iota(jnp.int32, (blocks, blocks), 0)
    stays = jnp.where(kept.astype(jnp.int32) == column, block, 0)
    source = source + jnp.sum(stays, axis=0, keepdims=True)
    table[0:8] = jnp.broadcast_to(source, (8, blocks))
    for k, first, _ in picks(going):
        table[8 * (k + 1) : 8 * (k + 2)] = jnp.broadcast_to(
            jnp.where(first < blocks, first, 0), (8, blocks)
        )


def prepare_own(tiles, home, away):
    centre = middle(tiles.shape[2])

    def prepare(r, carry):
        tile = tiles[r]
        here = tile[0:3] - centre
        square = jnp.sum(here * here, axis=0, keepdims=True)
        away[r] = far_rows(here, cube_root(tile[3:4]), square)
        home[r] = near_rows(here, square)
        return carry

    lax.fori_loop(0, tiles.shape[0], prepare, 0, unroll=16)


def prepare_ghosts(blocks, cap, ghost, away):
    centre = middle(ghost.shape[2])

    def prepare(places):
        for place in places:
            device = linear(place)
            for c in range(cap):
                tile = ghost[device, 4 * c : 4 * c + 4]
                here = tile[0:3] - centre
                square = jnp.sum(here * here, axis=0, keepdims=True)
                away[blocks + device * cap + c] = far_rows(here, cube_root(tile[3:4]), square)

    each_place(prepare)


def sum_densities(lookup, home, away, out, kept):
    columns, blocks = lookup.shape
    width = out.shape[1]
    again = blocks - kept.shape[0]

    def one_block(b, keep):
        rhs = home[b]
        acc = jnp.zeros((8, width), jnp.float32)
        for k in range(columns + 1):
            row = b if k == 0 else lookup[k - 1, b]
            w = jnp.dot(away[row], rhs, preferred_element_type=jnp.float32)
            w = jnp.maximum(w, 0.0)
            if keep:
                kept[b - again, k] = w
            w = w * w * w
            acc = acc + jnp.sum(w.reshape(w.shape[0] // 8, 8, width), axis=0)
        out[pl.ds(b, 1), :] = jnp.sum(acc, axis=0, keepdims=True)

    several(0, again, lambda b: one_block(b, False))
    several(again, blocks, lambda b: one_block(b, True))


def several(first, last, act):
    size = UNROLL
    while (last - first) % size:
        size //= 2

    def step(s, carry):
        for u in range(size):
            act(first + s * size + u)
        return carry

    lax.fori_loop(0, (last - first) // size, step, 0)


def moments(tile, q, centre):
    root = cube_root(tile[3:4])
    plain = jnp.concatenate([root, root * (tile[0:3] - centre)], axis=0)
    full = jnp.concatenate([plain, plain * q], axis=0)
    high = full.astype(jnp.bfloat16).astype(jnp.float32)
    return jnp.concatenate([high, full - high], axis=0).astype(jnp.bfloat16)


def own_moments(tiles, density, moment, term):
    centre = middle(tiles.shape[2])
    term[...] = pressure_term(density[...])

    def prepare(r, carry):
        moment[r] = moments(tiles[r], term[pl.ds(r, 1), :], centre)
        return carry

    lax.fori_loop(0, tiles.shape[0], prepare, 0, unroll=16)


def ghost_moments(blocks, ghost, ghost_density, moment):
    centre = middle(ghost.shape[2])
    cap = ghost_density.shape[1]

    def prepare(places):
        for place in places:
            device = linear(place)
            q = pressure_term(ghost_density[device])
            for c in range(cap):
                tile = ghost[device, 4 * c : 4 * c + 4]
                moment[blocks + device * cap + c] = moments(tile, q[c : c + 1], centre)

    each_place(prepare)


def sum_forces(lookup, home, away, tiles, moment, term, kept, finish):
    columns, blocks = lookup.shape
    width = tiles.shape[2]
    centre = middle(width)
    again = blocks - kept.shape[0]

    def one_block(b, keep):
        acc = jnp.zeros((16, 2 * width), jnp.float32)
        for k in range(columns + 1):
            row = b if k == 0 else lookup[k - 1, b]
            if keep:
                w = kept[b - again, k]
            else:
                w = jnp.dot(away[row], home[b], preferred_element_type=jnp.float32)
                w = jnp.maximum(w, 0.0)
            w = w * w
            high = w.astype(jnp.bfloat16)
            low = (w - high.astype(jnp.float32)).astype(jnp.bfloat16)
            both = jnp.concatenate([high, low], axis=1)
            acc = acc + jnp.dot(moment[row], both, preferred_element_type=jnp.float32)
        acc = acc[:, :width] + acc[:, width:]
        sums = acc[0:8] + acc[8:16]
        tile = tiles[b]
        here = tile[0:3] - centre
        near = here * sums[0:1] - sums[1:4]
        far = here * sums[4:5] - sums[5:8]
        finish(b, tile, 6.0 * INVERSE * (term[pl.ds(b, 1), :] * near + far))

    several(0, again, lambda b: one_block(b, False))
    several(again, blocks, lambda b: one_block(b, True))


def steps_kernel(
    rows_first,
    rows_second,
    lookup_first,
    lookup_second,
    points,
    velocity,
    mass,
    destination,
    points_out,
    speed_out,
    density_out,
    *scratch,
):
    (
        lookup_first_here,
        lookup_second_here,
        points_here,
        velocity_here,
        mass_here,
        destination_here,
        tiles,
        moved,
        ghost_first,
        ghost_second,
        send,
        thin_first,
        thin_second,
        thin_send,
        outbox,
        arrived,
        home,
        away,
        moment,
        term,
        density_first,
        kept,
        table,
        table_here,
        fetch_sem,
        table_sem,
        out_sem,
        in_sem,
        *pairs,
    ) = scratch
    cap, _ = rows_first.shape
    blocks = mass.shape[0]
    fetches = [
        pltpu.make_async_copy(source, target, fetch_sem.at[n])
        for n, (source, target) in enumerate(
            (
                (points, points_here),
                (velocity, velocity_here),
                (mass, mass_here),
                (destination, destination_here),
                (lookup_first, lookup_first_here),
                (lookup_second, lookup_second_here),
            )
        )
    ]
    for fetch in fetches:
        fetch.start()
    greet()
    me = linear(my_place())
    for land in (ghost_first, ghost_second, thin_first, thin_second):
        land[me] = jnp.ones(land.shape[1:], jnp.float32)
    for fetch in fetches:
        fetch.wait()

    def gather(r, carry):
        row = pl.ds(r, 1)
        for c in range(3):
            tiles[r, c : c + 1] = points_here[c, row, :]
            tiles[r, c + 4 : c + 5] = velocity_here[c, row, :]
        tiles[r, 3:4] = mass_here[row, :]
        tiles[r, 7:8] = mass_here[row, :]
        return carry

    lax.fori_loop(0, blocks, gather, 0, unroll=8)
    goal = jnp.broadcast_to(destination_here[...].astype(jnp.float32), (8, blocks))
    fill_points(rows_first, tiles, goal, send)
    meet()

    def one_step(rows, lookup, tiles, send, ghost, thin, density, sems, meanwhile, finish):
        swap_start(send, ghost, *sems[0:2])
        prepare_own(tiles, home, away)
        swap_wait(send, ghost, *sems[0:2])
        prepare_ghosts(blocks, cap, ghost, away)
        sum_densities(lookup, home, away, density, kept)
        fill_density(rows, density, thin_send)
        swap_start(thin_send, thin, *sems[2:4])
        own_moments(tiles, density, moment, term)
        meanwhile()
        swap_wait(thin_send, thin, *sems[2:4])
        ghost_moments(blocks, ghost, thin, moment)
        sum_forces(lookup, home, away, tiles, moment, term, kept, finish)

    def finish_first(b, tile, acceleration):
        speed = tile[4:7] + TIME_STEP * acceleration
        place = tile[0:3] + TIME_STEP * speed
        tiles[b] = jnp.concatenate([place, tile[3:4], speed, tile[3:4]], axis=0)

    def finish_second(b, tile, acceleration):
        speed = tile[4:7] + TIME_STEP * acceleration
        place = tile[0:3] + TIME_STEP * speed
        for c in range(3):
            speed_out[c, pl.ds(b, 1), :] = speed[c : c + 1]
            points_out[c, pl.ds(b, 1), :] = place[c : c + 1]

    def plan_moves():
        work_out_moves(destination_here, ghost_first, table, 4 * cap)
        copy = pltpu.make_async_copy(table, table_here, table_sem.at[0])
        copy.start()
        copy.wait()

    one_step(
        rows_first,
        lookup_first_here,
        tiles,
        send,
        ghost_first,
        thin_first,
        density_first,
        pairs[0:4],
        plan_moves,
        finish_first,
    )
    for face in range(6):
        for k in range(MOVE_CAP):
            outbox[face, k] = tiles[table_here[8 * (k + 1) + face, 0]]
    move_blocks(table_here, tiles, moved, outbox, arrived, out_sem, in_sem)
    narrow = send.at[:, pl.ds(0, 4 * cap)]
    fill_points(rows_second, moved, None, narrow)
    one_step(
        rows_second,
        lookup_second_here,
        moved,
        narrow,
        ghost_second,
        thin_second,
        density_out,
        pairs[4:8],
        lambda: None,
        finish_second,
    )


def padded_bytes(shape, dtype):
    *outer, rows, columns = shape
    size = -(-rows // 8) * 8 * -(-columns // 128) * 128 * jnp.dtype(dtype).itemsize
    for dim in outer:
        size *= dim
    return size


def per_device(
    position,
    velocity,
    particle_mass,
    send_first,
    neighbours_first,
    destination,
    send_second,
    neighbours_second,
):
    blocks, _, width = position.shape
    _, devices, cap = send_first.shape
    columns = neighbours_first.shape[1]
    total = blocks + devices * cap
    single, half = jnp.float32, jnp.bfloat16
    turn = lambda a: jnp.transpose(a, (1, 0, 2))
    given = [turn(position), turn(velocity), particle_mass, destination.reshape(1, blocks)]
    outs = [((3, blocks, width), single)] * 2 + [((blocks, width), single)]
    wide = (devices, 4 * cap + 8, width)
    thin = (devices, cap, width)
    box = (6, MOVE_CAP, 8, width)
    fixed = [
        *[(a.shape, a.dtype) for a in given],
        ((blocks, 8, width), single),
        ((blocks, 8, width), single),
        (wide, single),
        ((devices, 4 * cap, width), single),
        (wide, single),
        (thin, single),
        (thin, single),
        (thin, single),
        (box, single),
        (box, single),
        ((blocks, DEPTH, width), half),
        ((total, width, DEPTH), half),
        ((total, 16, width), half),
        ((blocks, width), single),
        ((blocks, width), single),
    ]
    each = padded_bytes((columns + 1, width, width), single)
    left = VMEM_PLAN - sum(padded_bytes(*entry) for entry in fixed + outs)
    kept = max(min(blocks, left // each) // UNROLL, 1) * UNROLL
    table = (8 * (MOVE_CAP + 1), blocks)
    smem = pl.BlockSpec(memory_space=pltpu.SMEM)
    hbm = pl.BlockSpec(memory_space=pltpu.HBM)
    vmem = pl.BlockSpec(memory_space=pltpu.VMEM)
    lookups = [neighbours_first.T, neighbours_second.T]
    position, velocity, density = pl.pallas_call(
        steps_kernel,
        out_shape=[jax.ShapeDtypeStruct(*entry) for entry in outs],
        in_specs=[smem] * 2 + [hbm] * (len(lookups) + len(given)),
        out_specs=[vmem] * len(outs),
        scratch_shapes=[
            *[pltpu.SMEM(a.shape, a.dtype) for a in lookups],
            *[pltpu.VMEM(*entry) for entry in fixed],
            pltpu.VMEM((kept, columns + 1, width, width), single),
            pltpu.VMEM(table, jnp.int32),
            pltpu.SMEM(table, jnp.int32),
            pltpu.SemaphoreType.DMA((len(lookups) + len(given),)),
            pltpu.SemaphoreType.DMA((1,)),
            pltpu.SemaphoreType.DMA((6,)),
            pltpu.SemaphoreType.DMA((6,)),
            *[pltpu.SemaphoreType.DMA((devices,))] * 8,
        ],
        compiler_params=pltpu.CompilerParams(
            vmem_limit_bytes=VMEM_LIMIT, collective_id=0, has_side_effects=True
        ),
    )(
        send_first[0].T,
        send_second[0].T,
        *[pltpu.with_memory_space_constraint(a, pltpu.HBM) for a in lookups + given],
    )
    return turn(position), turn(velocity), density


def solution(mesh):
    whole, flat = P(AXES, None, None), P(AXES, None)
    return jax.shard_map(
        per_device,
        mesh=mesh,
        in_specs=(whole, whole, flat, whole, flat, P(AXES), whole, flat),
        out_specs=(whole, whole, flat),
        check_vma=False,
    )
```

```python
import jax
import jax.numpy as jnp
from jax import lax
from jax.experimental import pallas as pl
from jax.experimental.pallas import tpu as pltpu
from jax.sharding import PartitionSpec as P

AXES = ("gx", "gy", "gz")
MOVE_CAP = 2
SMOOTH_LEN = 0.5
TIME_STEP = 0.25
INVERSE = 1.0 / (SMOOTH_LEN * SMOOTH_LEN)
PART_PAIRS = ((0, 0), (0, 1), (1, 0), (0, 2), (2, 0), (1, 1))
DEPTH = 8 * len(PART_PAIRS)
MESH = pl.DeviceIdType.MESH
UNROLL = 8
VMEM_LIMIT = 57 * 1024 * 1024
VMEM_PLAN = 57 * 1024 * 1024


def linear(place):
    size_y, size_z = lax.axis_size("gy"), lax.axis_size("gz")
    return (place[0] * size_y + place[1]) * size_z + place[2]


def my_place():
    return tuple(lax.axis_index(axis) for axis in AXES)


def shifted(shift):
    place = tuple(i + s for i, s in zip(my_place(), shift))
    inside = jnp.bool_(True)
    for i, axis in zip(place, AXES):
        inside = inside & (i >= 0) & (i < lax.axis_size(axis))
    return place, inside


def span(axis):
    i = lax.axis_index(axis)
    return jnp.maximum(i - 1, 0), jnp.minimum(i + 2, lax.axis_size(axis))


def each_place(act):
    (x_low, x_high), (y_low, y_high), (z_low, z_high) = (span(axis) for axis in AXES)
    size_z = lax.axis_size("gz")

    def along_y(y, x):
        act([(x, y, z_low + n) for n in range(min(size_z, 2))])
        if size_z > 2:
            pl.when(z_low + 2 < z_high)(lambda: act([(x, y, z_low + 2)]))
        return x

    def along_x(x, carry):
        lax.fori_loop(y_low, y_high, along_y, x)
        return carry

    lax.fori_loop(x_low, x_high, along_x, 0)


def each_neighbour(act):
    me = linear(my_place())

    def column(places):
        for place in places:
            pl.when(linear(place) != me)(lambda place=place: act(place))

    each_place(column)


def faces():
    found = []
    for axis in range(3):
        for step in (-1, 1):
            found.append(shifted(tuple(step if a == axis else 0 for a in range(3))))
    return found


def greet():
    barrier = pltpu.get_barrier_semaphore()

    def signal(place):
        pl.semaphore_signal(barrier, inc=1, device_id=place, device_id_type=MESH)

    each_neighbour(signal)


def meet():
    count = jnp.int32(1)
    for i, axis in zip(my_place(), AXES):
        size = lax.axis_size(axis)
        count = count * (1 + (i > 0).astype(jnp.int32) + (i < size - 1).astype(jnp.int32))
    pl.semaphore_wait(pltpu.get_barrier_semaphore(), count - 1)


def ghost_copy(send, land, send_sem, recv_sem, place, slot):
    to = linear(place)
    return pltpu.make_async_remote_copy(
        src_ref=send.at[to],
        dst_ref=land.at[slot],
        send_sem=send_sem.at[to],
        recv_sem=recv_sem.at[slot],
        device_id=place,
        device_id_type=MESH,
    )


def swap_start(send, land, send_sem, recv_sem):
    me = linear(my_place())
    each_neighbour(lambda place: ghost_copy(send, land, send_sem, recv_sem, place, me).start())


def swap_wait(send, land, send_sem, recv_sem):
    each_neighbour(
        lambda place: ghost_copy(send, land, send_sem, recv_sem, place, linear(place)).wait()
    )


def fill_points(rows, tiles, extra, send):
    cap = rows.shape[0]

    def fill(place):
        to = linear(place)
        for c in range(cap):
            send[to, 4 * c : 4 * c + 4] = tiles[jnp.maximum(rows[c, to], 0)][0:4]
        if extra is not None:
            send[to, 4 * cap : 4 * cap + 8] = extra

    each_neighbour(fill)


def fill_density(rows, density, send):
    def fill(place):
        to = linear(place)
        for c in range(rows.shape[0]):
            row = jnp.maximum(rows[c, to], 0)
            send[to, c : c + 1] = density[pl.ds(row, 1), :]

    each_neighbour(fill)


def move_blocks(table, tiles, moved, outbox, arrived, out_sem, in_sem):
    blocks = tiles.shape[0]

    def block_copy(face, place, slot):
        return pltpu.make_async_remote_copy(
            src_ref=outbox.at[face],
            dst_ref=arrived.at[slot],
            send_sem=out_sem.at[face],
            recv_sem=in_sem.at[slot],
            device_id=place,
            device_id_type=MESH,
        )

    for face, (place, inside) in enumerate(faces()):
        pl.when(inside)(lambda: block_copy(face, place, face ^ 1).start())
    for face, (place, inside) in enumerate(faces()):
        pl.when(inside)(lambda: block_copy(face, place, face).wait())

    def settle(p, carry):
        source = table[0, p]
        kept = tiles[jnp.minimum(source, blocks - 1)]
        slot = jnp.maximum(source - blocks, 0)
        came = arrived[slot // MOVE_CAP, slot % MOVE_CAP]
        moved[p] = jnp.where(source < blocks, kept, came)
        return carry

    lax.fori_loop(0, blocks, settle, 0, unroll=8)


def pressure_term(density):
    return jnp.exp(jnp.log(density) * (-1.0 / 3.0))


def cube_root(mass):
    return jnp.exp(jnp.log(mass) * (1.0 / 3.0))


def three_parts(value):
    parts = []
    for _ in range(3):
        part = value.astype(jnp.bfloat16).astype(jnp.float32)
        parts.append(part)
        value = value - part
    return parts


def middle(width):
    row = lax.broadcasted_iota(jnp.int32, (3, width), 0)
    place = [i.astype(jnp.float32) + 0.5 for i in my_place()]
    return jnp.where(row == 0, place[0], jnp.where(row == 1, place[1], place[2]))


def far_rows(here, root, square):
    blank = jnp.zeros_like(here)
    far = jnp.concatenate(
        [2.0 * INVERSE * root * here, -INVERSE * root * square, root, blank], axis=0
    )
    parts = three_parts(far)
    return jnp.concatenate([parts[a] for a, _ in PART_PAIRS], axis=0).T.astype(jnp.bfloat16)


def near_rows(here, square):
    near = jnp.concatenate(
        [here, jnp.ones_like(square), 1.0 - INVERSE * square, jnp.zeros_like(here)], axis=0
    )
    parts = three_parts(near)
    return jnp.concatenate([parts[b] for _, b in PART_PAIRS], axis=0).astype(jnp.bfloat16)


def work_out_moves(destination, ghost, table, at):
    blocks = destination.shape[1]
    me = linear(my_place())
    goal = destination[...]
    lane = lax.broadcasted_iota(jnp.int32, (8, blocks), 1)
    face = lax.broadcasted_iota(jnp.int32, (8, blocks), 0)
    theirs, targets = [], []
    for place, inside in faces():
        device = jnp.where(inside, linear(place), -1)
        row = ghost[jnp.maximum(device, 0), at : at + 1].astype(jnp.int32)
        theirs.append(jnp.where(inside, row, -1))
        targets.append(jnp.full((1, blocks), device, jnp.int32))
    theirs += [jnp.full((2, blocks), -1, jnp.int32)]
    targets += [jnp.full((2, blocks), -1, jnp.int32)]
    coming = jnp.concatenate(theirs, axis=0) - me * blocks
    going = goal - jnp.concatenate(targets, axis=0) * blocks

    def picks(offset):
        left = (offset >= 0) & (offset < blocks)
        for k in range(MOVE_CAP):
            first = jnp.min(jnp.where(left, lane, blocks), axis=1, keepdims=True)
            hit = left & (lane == first)
            left = left & (lane != first)
            yield k, first, hit

    source = jnp.zeros((8, blocks), jnp.int32)
    for k, first, hit in picks(coming):
        spot = jnp.sum(jnp.where(hit, coming, 0), axis=1, keepdims=True)
        spot = jnp.where(first < blocks, spot, -1)
        source = source + jnp.where(lane == spot, blocks + face * MOVE_CAP + k, 0)
    source = jnp.sum(source, axis=0, keepdims=True)
    kept = jnp.broadcast_to((goal - me * blocks).astype(jnp.float32), (blocks, blocks)).T
    column = lax.broadcasted_iota(jnp.int32, (blocks, blocks), 1)
    block = lax.broadcasted_iota(jnp.int32, (blocks, blocks), 0)
    stays = jnp.where(kept.astype(jnp.int32) == column, block, 0)
    source = source + jnp.sum(stays, axis=0, keepdims=True)
    table[0:8] = jnp.broadcast_to(source, (8, blocks))
    for k, first, _ in picks(going):
        table[8 * (k + 1) : 8 * (k + 2)] = jnp.broadcast_to(
            jnp.where(first < blocks, first, 0), (8, blocks)
        )


def prepare_own(tiles, home, away):
    centre = middle(tiles.shape[2])

    def prepare(r, carry):
        tile = tiles[r]
        here = tile[0:3] - centre
        square = jnp.sum(here * here, axis=0, keepdims=True)
        away[r] = far_rows(here, cube_root(tile[3:4]), square)
        home[r] = near_rows(here, square)
        return carry

    lax.fori_loop(0, tiles.shape[0], prepare, 0, unroll=16)


def prepare_ghosts(blocks, cap, ghost, away):
    centre = middle(ghost.shape[2])

    def prepare(places):
        for place in places:
            device = linear(place)
            for c in range(cap):
                tile = ghost[device, 4 * c : 4 * c + 4]
                here = tile[0:3] - centre
                square = jnp.sum(here * here, axis=0, keepdims=True)
                away[blocks + device * cap + c] = far_rows(here, cube_root(tile[3:4]), square)

    each_place(prepare)


def groups(blocks, kept):
    slots = kept.shape[0]
    return min(slots, blocks - slots) // UNROLL * UNROLL, blocks - slots


def sum_densities(lookup, home, away, out, kept, store, store_sem):
    columns, blocks = lookup.shape
    width = out.shape[1]
    far_end, near_start = groups(blocks, kept)

    def one_block(b, slot):
        rhs = home[b]
        acc = jnp.zeros((8, width), jnp.float32)
        for k in range(columns + 1):
            row = b if k == 0 else lookup[k - 1, b]
            w = jnp.dot(away[row], rhs, preferred_element_type=jnp.float32)
            w = jnp.maximum(w, 0.0)
            square = w * w
            if slot is not None:
                kept[slot, k] = square
            w = square * w
            acc = acc + jnp.sum(w.reshape(w.shape[0] // 8, 8, width), axis=0)
        out[pl.ds(b, 1), :] = jnp.sum(acc, axis=0, keepdims=True)

    def put(slot):
        return pltpu.make_async_copy(kept.at[slot], store.at[slot], store_sem.at[slot])

    def far(some):
        for b in some:
            one_block(b, b)
        for b in some:
            put(b).start()

    def plain(some):
        for b in some:
            one_block(b, None)

    def near(some):
        for b in some:
            one_block(b, b - near_start)

    def near_again(some):
        for b in some:
            put(b - near_start).wait()
        near(some)

    several(0, far_end, far)
    several(far_end, near_start, plain)
    several(near_start, near_start + far_end, near_again)
    several(near_start + far_end, blocks, near)


def several(first, last, act):
    size = UNROLL
    while (last - first) % size:
        size //= 2

    def step(s, carry):
        act([first + s * size + u for u in range(size)])
        return carry

    lax.fori_loop(0, (last - first) // size, step, 0)


def moments(tile, q, centre):
    root = cube_root(tile[3:4])
    plain = jnp.concatenate([root, root * (tile[0:3] - centre)], axis=0)
    full = jnp.concatenate([plain, plain * q], axis=0)
    high = full.astype(jnp.bfloat16).astype(jnp.float32)
    return jnp.concatenate([high, full - high], axis=0).astype(jnp.bfloat16)


def own_moments(tiles, density, moment, term):
    centre = middle(tiles.shape[2])
    term[...] = pressure_term(density[...])

    def prepare(r, carry):
        moment[r] = moments(tiles[r], term[pl.ds(r, 1), :], centre)
        return carry

    lax.fori_loop(0, tiles.shape[0], prepare, 0, unroll=16)


def ghost_moments(blocks, ghost, ghost_density, moment):
    centre = middle(ghost.shape[2])
    cap = ghost_density.shape[1]

    def prepare(places):
        for place in places:
            device = linear(place)
            q = pressure_term(ghost_density[device])
            for c in range(cap):
                tile = ghost[device, 4 * c : 4 * c + 4]
                moment[blocks + device * cap + c] = moments(tile, q[c : c + 1], centre)

    each_place(prepare)


def sum_forces(lookup, home, away, tiles, moment, term, kept, store, store_sem, finish):
    columns, blocks = lookup.shape
    width = tiles.shape[2]
    centre = middle(width)
    far_end, near_start = groups(blocks, kept)

    def one_block(b, slot):
        acc = jnp.zeros((16, 2 * width), jnp.float32)
        for k in range(columns + 1):
            row = b if k == 0 else lookup[k - 1, b]
            if slot is None:
                w = jnp.dot(away[row], home[b], preferred_element_type=jnp.float32)
                w = jnp.maximum(w, 0.0)
                square = w * w
            else:
                square = kept[slot, k]
            high = square.astype(jnp.bfloat16)
            low = (square - high.astype(jnp.float32)).astype(jnp.bfloat16)
            both = jnp.concatenate([high, low], axis=1)
            acc = acc + jnp.dot(moment[row], both, preferred_element_type=jnp.float32)
        acc = acc[:, :width] + acc[:, width:]
        sums = acc[0:8] + acc[8:16]
        tile = tiles[b]
        here = tile[0:3] - centre
        near = here * sums[0:1] - sums[1:4]
        far = here * sums[4:5] - sums[5:8]
        finish(b, tile, 6.0 * INVERSE * (term[pl.ds(b, 1), :] * near + far))

    def get(slot):
        return pltpu.make_async_copy(store.at[slot], kept.at[slot], store_sem.at[slot])

    def near(some):
        for b in some:
            one_block(b, b - near_start)

    def near_then_get(some):
        near(some)
        for b in some:
            get(b - near_start).start()

    def plain(some):
        for b in some:
            one_block(b, None)

    def far(some):
        for b in some:
            get(b).wait()
        for b in some:
            one_block(b, b)

    several(near_start, near_start + far_end, near_then_get)
    several(near_start + far_end, blocks, near)
    several(far_end, near_start, plain)
    several(0, far_end, far)


def steps_kernel(
    rows_first,
    rows_second,
    lookup_first,
    lookup_second,
    points,
    velocity,
    mass,
    destination,
    points_out,
    speed_out,
    density_out,
    store,
    *scratch,
):
    (
        lookup_first_here,
        lookup_second_here,
        points_here,
        velocity_here,
        mass_here,
        destination_here,
        tiles,
        moved,
        ghost_first,
        ghost_second,
        send,
        thin_first,
        thin_second,
        thin_send,
        outbox,
        arrived,
        home,
        away,
        moment,
        term,
        density_first,
        kept,
        store_sem,
        table,
        table_here,
        fetch_sem,
        table_sem,
        out_sem,
        in_sem,
        *pairs,
    ) = scratch
    cap, _ = rows_first.shape
    blocks = mass.shape[0]
    fetches = [
        pltpu.make_async_copy(source, target, fetch_sem.at[n])
        for n, (source, target) in enumerate(
            (
                (points, points_here),
                (velocity, velocity_here),
                (mass, mass_here),
                (destination, destination_here),
                (lookup_first, lookup_first_here),
                (lookup_second, lookup_second_here),
            )
        )
    ]
    for fetch in fetches:
        fetch.start()
    greet()
    me = linear(my_place())
    for land in (ghost_first, ghost_second, thin_first, thin_second):
        land[me] = jnp.ones(land.shape[1:], jnp.float32)
    for fetch in fetches:
        fetch.wait()

    def gather(r, carry):
        row = pl.ds(r, 1)
        for c in range(3):
            tiles[r, c : c + 1] = points_here[c, row, :]
            tiles[r, c + 4 : c + 5] = velocity_here[c, row, :]
        tiles[r, 3:4] = mass_here[row, :]
        tiles[r, 7:8] = mass_here[row, :]
        return carry

    lax.fori_loop(0, blocks, gather, 0, unroll=8)
    goal = jnp.broadcast_to(destination_here[...].astype(jnp.float32), (8, blocks))
    fill_points(rows_first, tiles, goal, send)
    meet()

    def one_step(rows, lookup, tiles, send, ghost, thin, density, sems, meanwhile, finish):
        swap_start(send, ghost, *sems[0:2])
        prepare_own(tiles, home, away)
        swap_wait(send, ghost, *sems[0:2])
        prepare_ghosts(blocks, cap, ghost, away)
        sum_densities(lookup, home, away, density, kept, store, store_sem)
        fill_density(rows, density, thin_send)
        swap_start(thin_send, thin, *sems[2:4])
        own_moments(tiles, density, moment, term)
        meanwhile()
        swap_wait(thin_send, thin, *sems[2:4])
        ghost_moments(blocks, ghost, thin, moment)
        sum_forces(lookup, home, away, tiles, moment, term, kept, store, store_sem, finish)

    def finish_first(b, tile, acceleration):
        speed = tile[4:7] + TIME_STEP * acceleration
        place = tile[0:3] + TIME_STEP * speed
        tiles[b] = jnp.concatenate([place, tile[3:4], speed, tile[3:4]], axis=0)

    def finish_second(b, tile, acceleration):
        speed = tile[4:7] + TIME_STEP * acceleration
        place = tile[0:3] + TIME_STEP * speed
        for c in range(3):
            speed_out[c, pl.ds(b, 1), :] = speed[c : c + 1]
            points_out[c, pl.ds(b, 1), :] = place[c : c + 1]

    def plan_moves():
        work_out_moves(destination_here, ghost_first, table, 4 * cap)
        copy = pltpu.make_async_copy(table, table_here, table_sem.at[0])
        copy.start()
        copy.wait()

    one_step(
        rows_first,
        lookup_first_here,
        tiles,
        send,
        ghost_first,
        thin_first,
        density_first,
        pairs[0:4],
        plan_moves,
        finish_first,
    )
    for face in range(6):
        for k in range(MOVE_CAP):
            outbox[face, k] = tiles[table_here[8 * (k + 1) + face, 0]]
    move_blocks(table_here, tiles, moved, outbox, arrived, out_sem, in_sem)
    narrow = send.at[:, pl.ds(0, 4 * cap)]
    fill_points(rows_second, moved, None, narrow)
    one_step(
        rows_second,
        lookup_second_here,
        moved,
        narrow,
        ghost_second,
        thin_second,
        density_out,
        pairs[4:8],
        lambda: None,
        finish_second,
    )


def padded_bytes(shape, dtype):
    *outer, rows, columns = shape
    size = -(-rows // 8) * 8 * -(-columns // 128) * 128 * jnp.dtype(dtype).itemsize
    for dim in outer:
        size *= dim
    return size


def per_device(
    position,
    velocity,
    particle_mass,
    send_first,
    neighbours_first,
    destination,
    send_second,
    neighbours_second,
):
    blocks, _, width = position.shape
    _, devices, cap = send_first.shape
    columns = neighbours_first.shape[1]
    total = blocks + devices * cap
    single, half = jnp.float32, jnp.bfloat16
    turn = lambda a: jnp.transpose(a, (1, 0, 2))
    given = [turn(position), turn(velocity), particle_mass, destination.reshape(1, blocks)]
    outs = [((3, blocks, width), single)] * 2 + [((blocks, width), single)]
    wide = (devices, 4 * cap + 8, width)
    thin = (devices, cap, width)
    box = (6, MOVE_CAP, 8, width)
    fixed = [
        *[(a.shape, a.dtype) for a in given],
        ((blocks, 8, width), single),
        ((blocks, 8, width), single),
        (wide, single),
        ((devices, 4 * cap, width), single),
        (wide, single),
        (thin, single),
        (thin, single),
        (thin, single),
        (box, single),
        (box, single),
        ((blocks, DEPTH, width), half),
        ((total, width, DEPTH), half),
        ((total, 16, width), half),
        ((blocks, width), single),
        ((blocks, width), single),
    ]
    each = padded_bytes((columns + 1, width, width), single)
    left = VMEM_PLAN - sum(padded_bytes(*entry) for entry in fixed + outs)
    kept = max(min(blocks, left // each) // UNROLL, 1) * UNROLL
    weights = (kept, columns + 1, width, width)
    table = (8 * (MOVE_CAP + 1), blocks)
    smem = pl.BlockSpec(memory_space=pltpu.SMEM)
    hbm = pl.BlockSpec(memory_space=pltpu.HBM)
    vmem = pl.BlockSpec(memory_space=pltpu.VMEM)
    lookups = [neighbours_first.T, neighbours_second.T]
    position, velocity, density, _ = pl.pallas_call(
        steps_kernel,
        out_shape=[pltpu.VMEM(*entry) for entry in outs] + [jax.ShapeDtypeStruct(weights, single)],
        in_specs=[smem] * 2 + [hbm] * (len(lookups) + len(given)),
        out_specs=[vmem] * len(outs) + [hbm],
        scratch_shapes=[
            *[pltpu.SMEM(a.shape, a.dtype) for a in lookups],
            *[pltpu.VMEM(*entry) for entry in fixed],
            pltpu.VMEM(weights, single),
            pltpu.SemaphoreType.DMA((kept,)),
            pltpu.VMEM(table, jnp.int32),
            pltpu.SMEM(table, jnp.int32),
            pltpu.SemaphoreType.DMA((len(lookups) + len(given),)),
            pltpu.SemaphoreType.DMA((1,)),
            pltpu.SemaphoreType.DMA((6,)),
            pltpu.SemaphoreType.DMA((6,)),
            *[pltpu.SemaphoreType.DMA((devices,))] * 8,
        ],
        compiler_params=pltpu.CompilerParams(
            vmem_limit_bytes=VMEM_LIMIT, collective_id=0, has_side_effects=True
        ),
    )(
        send_first[0].T,
        send_second[0].T,
        *[pltpu.with_memory_space_constraint(a, pltpu.HBM) for a in lookups + given],
    )
    return turn(position), turn(velocity), density


def solution(mesh):
    whole, flat = P(AXES, None, None), P(AXES, None)
    return jax.shard_map(
        per_device,
        mesh=mesh,
        in_specs=(whole, whole, flat, whole, flat, P(AXES), whole, flat),
        out_specs=(whole, whole, flat),
        check_vma=False,
    )
```

```python
import jax
import jax.numpy as jnp
from jax import lax
from jax.experimental import pallas as pl
from jax.experimental.pallas import tpu as pltpu
from jax.sharding import PartitionSpec as P

AXES = ("gx", "gy", "gz")
MOVE_CAP = 2
SMOOTH_LEN = 0.5
TIME_STEP = 0.25
INVERSE = 1.0 / (SMOOTH_LEN * SMOOTH_LEN)
PART_PAIRS = ((0, 0), (0, 1), (1, 0), (0, 2), (2, 0), (1, 1))
DEPTH = 8 * len(PART_PAIRS)
MESH = pl.DeviceIdType.MESH
UNROLL = 8
SECOND = 16
VMEM_LIMIT = 57 * 1024 * 1024
VMEM_PLAN = 57 * 1024 * 1024


def linear(place):
    size_y, size_z = lax.axis_size("gy"), lax.axis_size("gz")
    return (place[0] * size_y + place[1]) * size_z + place[2]


def my_place():
    return tuple(lax.axis_index(axis) for axis in AXES)


def shifted(shift):
    place = tuple(i + s for i, s in zip(my_place(), shift))
    inside = jnp.bool_(True)
    for i, axis in zip(place, AXES):
        inside = inside & (i >= 0) & (i < lax.axis_size(axis))
    return place, inside


def span(axis):
    i = lax.axis_index(axis)
    return jnp.maximum(i - 1, 0), jnp.minimum(i + 2, lax.axis_size(axis))


def each_place(act):
    (x_low, x_high), (y_low, y_high), (z_low, z_high) = (span(axis) for axis in AXES)
    size_z = lax.axis_size("gz")

    def along_y(y, x):
        act([(x, y, z_low + n) for n in range(min(size_z, 2))])
        if size_z > 2:
            pl.when(z_low + 2 < z_high)(lambda: act([(x, y, z_low + 2)]))
        return x

    def along_x(x, carry):
        lax.fori_loop(y_low, y_high, along_y, x)
        return carry

    lax.fori_loop(x_low, x_high, along_x, 0)


def each_neighbour(act):
    me = linear(my_place())

    def column(places):
        for place in places:
            pl.when(linear(place) != me)(lambda place=place: act(place))

    each_place(column)


def faces():
    found = []
    for axis in range(3):
        for step in (-1, 1):
            found.append(shifted(tuple(step if a == axis else 0 for a in range(3))))
    return found


def greet():
    barrier = pltpu.get_barrier_semaphore()

    def signal(place):
        pl.semaphore_signal(barrier, inc=1, device_id=place, device_id_type=MESH)

    each_neighbour(signal)


def meet():
    count = jnp.int32(1)
    for i, axis in zip(my_place(), AXES):
        size = lax.axis_size(axis)
        count = count * (1 + (i > 0).astype(jnp.int32) + (i < size - 1).astype(jnp.int32))
    pl.semaphore_wait(pltpu.get_barrier_semaphore(), count - 1)


def ghost_copy(send, land, send_sem, recv_sem, place, slot):
    to = linear(place)
    return pltpu.make_async_remote_copy(
        src_ref=send.at[to],
        dst_ref=land.at[slot],
        send_sem=send_sem.at[to],
        recv_sem=recv_sem.at[slot],
        device_id=place,
        device_id_type=MESH,
    )


def swap_start(send, land, send_sem, recv_sem):
    me = linear(my_place())
    each_neighbour(lambda place: ghost_copy(send, land, send_sem, recv_sem, place, me).start())


def swap_wait(send, land, send_sem, recv_sem):
    each_neighbour(
        lambda place: ghost_copy(send, land, send_sem, recv_sem, place, linear(place)).wait()
    )


def fill_points(rows, tiles, extra, send):
    cap = rows.shape[0]

    def fill(place):
        to = linear(place)
        for c in range(cap):
            send[to, 4 * c : 4 * c + 4] = tiles[jnp.maximum(rows[c, to], 0)][0:4]
        if extra is not None:
            send[to, 4 * cap : 4 * cap + 8] = extra

    each_neighbour(fill)


def fill_density(rows, density, send):
    def fill(place):
        to = linear(place)
        for c in range(rows.shape[0]):
            row = jnp.maximum(rows[c, to], 0)
            send[to, c : c + 1] = density[pl.ds(row, 1), :]

    each_neighbour(fill)


def move_blocks(table, tiles, moved, outbox, arrived, out_sem, in_sem):
    blocks = tiles.shape[0]

    def block_copy(face, place, slot):
        return pltpu.make_async_remote_copy(
            src_ref=outbox.at[face],
            dst_ref=arrived.at[slot],
            send_sem=out_sem.at[face],
            recv_sem=in_sem.at[slot],
            device_id=place,
            device_id_type=MESH,
        )

    for face, (place, inside) in enumerate(faces()):
        pl.when(inside)(lambda: block_copy(face, place, face ^ 1).start())
    for face, (place, inside) in enumerate(faces()):
        pl.when(inside)(lambda: block_copy(face, place, face).wait())

    def settle(p, carry):
        source = table[0, p]
        kept = tiles[jnp.minimum(source, blocks - 1)]
        slot = jnp.maximum(source - blocks, 0)
        came = arrived[slot // MOVE_CAP, slot % MOVE_CAP]
        moved[p] = jnp.where(source < blocks, kept, came)
        return carry

    lax.fori_loop(0, blocks, settle, 0, unroll=8)


def pressure_term(density):
    return jnp.exp(jnp.log(density) * (-1.0 / 3.0))


def cube_root(mass):
    return jnp.exp(jnp.log(mass) * (1.0 / 3.0))


def three_parts(value):
    parts = []
    for _ in range(3):
        part = value.astype(jnp.bfloat16).astype(jnp.float32)
        parts.append(part)
        value = value - part
    return parts


def middle(width):
    row = lax.broadcasted_iota(jnp.int32, (3, width), 0)
    place = [i.astype(jnp.float32) + 0.5 for i in my_place()]
    return jnp.where(row == 0, place[0], jnp.where(row == 1, place[1], place[2]))


def far_rows(here, root, square):
    blank = jnp.zeros_like(here)
    far = jnp.concatenate(
        [2.0 * INVERSE * root * here, -INVERSE * root * square, root, blank], axis=0
    )
    parts = three_parts(far)
    return jnp.concatenate([parts[a] for a, _ in PART_PAIRS], axis=0).T.astype(jnp.bfloat16)


def near_rows(here, square):
    near = jnp.concatenate(
        [here, jnp.ones_like(square), 1.0 - INVERSE * square, jnp.zeros_like(here)], axis=0
    )
    parts = three_parts(near)
    return jnp.concatenate([parts[b] for _, b in PART_PAIRS], axis=0).astype(jnp.bfloat16)


def work_out_moves(destination, ghost, table, at):
    blocks = destination.shape[1]
    me = linear(my_place())
    goal = destination[...]
    lane = lax.broadcasted_iota(jnp.int32, (8, blocks), 1)
    face = lax.broadcasted_iota(jnp.int32, (8, blocks), 0)
    theirs, targets = [], []
    for place, inside in faces():
        device = jnp.where(inside, linear(place), -1)
        row = ghost[jnp.maximum(device, 0), at : at + 1].astype(jnp.int32)
        theirs.append(jnp.where(inside, row, -1))
        targets.append(jnp.full((1, blocks), device, jnp.int32))
    theirs += [jnp.full((2, blocks), -1, jnp.int32)]
    targets += [jnp.full((2, blocks), -1, jnp.int32)]
    coming = jnp.concatenate(theirs, axis=0) - me * blocks
    going = goal - jnp.concatenate(targets, axis=0) * blocks

    def picks(offset):
        left = (offset >= 0) & (offset < blocks)
        for k in range(MOVE_CAP):
            first = jnp.min(jnp.where(left, lane, blocks), axis=1, keepdims=True)
            hit = left & (lane == first)
            left = left & (lane != first)
            yield k, first, hit

    source = jnp.zeros((8, blocks), jnp.int32)
    for k, first, hit in picks(coming):
        spot = jnp.sum(jnp.where(hit, coming, 0), axis=1, keepdims=True)
        spot = jnp.where(first < blocks, spot, -1)
        source = source + jnp.where(lane == spot, blocks + face * MOVE_CAP + k, 0)
    source = jnp.sum(source, axis=0, keepdims=True)
    kept = jnp.broadcast_to((goal - me * blocks).astype(jnp.float32), (blocks, blocks)).T
    column = lax.broadcasted_iota(jnp.int32, (blocks, blocks), 1)
    block = lax.broadcasted_iota(jnp.int32, (blocks, blocks), 0)
    stays = jnp.where(kept.astype(jnp.int32) == column, block, 0)
    source = source + jnp.sum(stays, axis=0, keepdims=True)
    table[0:8] = jnp.broadcast_to(source, (8, blocks))
    for k, first, _ in picks(going):
        table[8 * (k + 1) : 8 * (k + 2)] = jnp.broadcast_to(
            jnp.where(first < blocks, first, 0), (8, blocks)
        )


def prepare_own(tiles, home, away):
    centre = middle(tiles.shape[2])

    def prepare(r, carry):
        tile = tiles[r]
        here = tile[0:3] - centre
        square = jnp.sum(here * here, axis=0, keepdims=True)
        away[r] = far_rows(here, cube_root(tile[3:4]), square)
        home[r] = near_rows(here, square)
        return carry

    lax.fori_loop(0, tiles.shape[0], prepare, 0, unroll=16)


def prepare_ghosts(blocks, cap, ghost, away):
    centre = middle(ghost.shape[2])

    def prepare(places):
        for place in places:
            device = linear(place)
            for c in range(cap):
                tile = ghost[device, 4 * c : 4 * c + 4]
                here = tile[0:3] - centre
                square = jnp.sum(here * here, axis=0, keepdims=True)
                away[blocks + device * cap + c] = far_rows(here, cube_root(tile[3:4]), square)

    each_place(prepare)


def groups(blocks, kept, store):
    slots, far = kept.shape[0], store.shape[0]
    first = min(slots, far)
    near = blocks - slots
    second = near - (far - first)
    return (0, first), (second, near), (first, second), (near, blocks)


def sum_densities(lookup, home, away, out, kept, store, store_sem):
    columns, blocks = lookup.shape
    width = out.shape[1]
    once, twice, rest, last = groups(blocks, kept, store)
    second = twice[1] - twice[0]

    def one_block(b, slot):
        rhs = home[b]
        acc = jnp.zeros((8, width), jnp.float32)
        for k in range(columns + 1):
            row = b if k == 0 else lookup[k - 1, b]
            w = jnp.dot(away[row], rhs, preferred_element_type=jnp.float32)
            w = jnp.maximum(w, 0.0)
            square = w * w
            if slot is not None:
                kept[slot, k] = square
            w = square * w
            acc = acc + jnp.sum(w.reshape(w.shape[0] // 8, 8, width), axis=0)
        out[pl.ds(b, 1), :] = jnp.sum(acc, axis=0, keepdims=True)

    def put(slot, entry):
        return pltpu.make_async_copy(kept.at[slot], store.at[entry], store_sem.at[entry])

    def far_once(some):
        for b in some:
            one_block(b, b)
        for b in some:
            put(b, b).start()

    def far_twice(some):
        for b in some:
            put(b - twice[0], b - twice[0]).wait()
        for b in some:
            one_block(b, b - twice[0])
        for b in some:
            put(b - twice[0], b - twice[0] + once[1]).start()

    def plain(some):
        for b in some:
            one_block(b, None)

    def near(entry_of):
        def act(some):
            for b in some:
                put(b - last[0], entry_of(b - last[0])).wait()
            for b in some:
                one_block(b, b - last[0])

        return act

    several(*once, far_once)
    several(*rest, plain)
    several(*twice, far_twice)
    several(last[0] + second, last[0] + once[1], near(lambda slot: slot))
    several(last[0], last[0] + second, near(lambda slot: slot + once[1]))
    several(last[0] + once[1], last[1], lambda some: [one_block(b, b - last[0]) for b in some])


def several(first, last, act):
    if first == last:
        return
    size = UNROLL
    while (last - first) % size:
        size //= 2

    def step(s, carry):
        act([first + s * size + u for u in range(size)])
        return carry

    lax.fori_loop(0, (last - first) // size, step, 0)


def moments(tile, q, centre):
    root = cube_root(tile[3:4])
    plain = jnp.concatenate([root, root * (tile[0:3] - centre)], axis=0)
    full = jnp.concatenate([plain, plain * q], axis=0)
    high = full.astype(jnp.bfloat16).astype(jnp.float32)
    return jnp.concatenate([high, full - high], axis=0).astype(jnp.bfloat16)


def own_moments(tiles, density, moment, term):
    centre = middle(tiles.shape[2])
    term[...] = pressure_term(density[...])

    def prepare(r, carry):
        moment[r] = moments(tiles[r], term[pl.ds(r, 1), :], centre)
        return carry

    lax.fori_loop(0, tiles.shape[0], prepare, 0, unroll=16)


def ghost_moments(blocks, ghost, ghost_density, moment):
    centre = middle(ghost.shape[2])
    cap = ghost_density.shape[1]

    def prepare(places):
        for place in places:
            device = linear(place)
            q = pressure_term(ghost_density[device])
            for c in range(cap):
                tile = ghost[device, 4 * c : 4 * c + 4]
                moment[blocks + device * cap + c] = moments(tile, q[c : c + 1], centre)

    each_place(prepare)


def sum_forces(lookup, home, away, tiles, moment, term, kept, store, store_sem, finish):
    columns, blocks = lookup.shape
    width = tiles.shape[2]
    centre = middle(width)
    once, twice, rest, last = groups(blocks, kept, store)
    second = twice[1] - twice[0]

    def one_block(b, slot):
        acc = jnp.zeros((16, 2 * width), jnp.float32)
        for k in range(columns + 1):
            row = b if k == 0 else lookup[k - 1, b]
            if slot is None:
                w = jnp.dot(away[row], home[b], preferred_element_type=jnp.float32)
                w = jnp.maximum(w, 0.0)
                square = w * w
            else:
                square = kept[slot, k]
            high = square.astype(jnp.bfloat16)
            low = (square - high.astype(jnp.float32)).astype(jnp.bfloat16)
            both = jnp.concatenate([high, low], axis=1)
            acc = acc + jnp.dot(moment[row], both, preferred_element_type=jnp.float32)
        acc = acc[:, :width] + acc[:, width:]
        sums = acc[0:8] + acc[8:16]
        tile = tiles[b]
        here = tile[0:3] - centre
        near = here * sums[0:1] - sums[1:4]
        far = here * sums[4:5] - sums[5:8]
        finish(b, tile, 6.0 * INVERSE * (term[pl.ds(b, 1), :] * near + far))

    def get(slot, entry):
        return pltpu.make_async_copy(store.at[entry], kept.at[slot], store_sem.at[entry])

    def near(some):
        for b in some:
            one_block(b, b - last[0])

    def near_then_get(some):
        near(some)
        for b in some:
            get(b - last[0], b - last[0]).start()

    def plain(some):
        for b in some:
            one_block(b, None)

    def far_once(some):
        for b in some:
            get(b, b).wait()
        for b in some:
            one_block(b, b)

    def far_once_then_get(some):
        far_once(some)
        for b in some:
            get(b, b + once[1]).start()

    def far_twice(some):
        for b in some:
            get(b - twice[0], b - twice[0] + once[1]).wait()
        for b in some:
            one_block(b, b - twice[0])

    several(last[0] + once[1], last[1], near)
    several(last[0], last[0] + once[1], near_then_get)
    several(*rest, plain)
    several(0, second, far_once_then_get)
    several(second, once[1], far_once)
    several(*twice, far_twice)


def steps_kernel(
    rows_first,
    rows_second,
    lookup_first,
    lookup_second,
    points,
    velocity,
    mass,
    destination,
    points_out,
    speed_out,
    density_out,
    store,
    *scratch,
):
    (
        lookup_first_here,
        lookup_second_here,
        points_here,
        velocity_here,
        mass_here,
        destination_here,
        tiles,
        moved,
        ghost_first,
        ghost_second,
        send,
        thin_first,
        thin_second,
        thin_send,
        outbox,
        arrived,
        home,
        away,
        moment,
        term,
        density_first,
        kept,
        store_sem,
        table,
        table_here,
        fetch_sem,
        table_sem,
        out_sem,
        in_sem,
        *pairs,
    ) = scratch
    cap, _ = rows_first.shape
    blocks = mass.shape[0]
    fetches = [
        pltpu.make_async_copy(source, target, fetch_sem.at[n])
        for n, (source, target) in enumerate(
            (
                (points, points_here),
                (velocity, velocity_here),
                (mass, mass_here),
                (destination, destination_here),
                (lookup_first, lookup_first_here),
                (lookup_second, lookup_second_here),
            )
        )
    ]
    for fetch in fetches:
        fetch.start()
    greet()
    me = linear(my_place())
    for land in (ghost_first, ghost_second, thin_first, thin_second):
        land[me] = jnp.ones(land.shape[1:], jnp.float32)
    for fetch in fetches:
        fetch.wait()

    def gather(r, carry):
        row = pl.ds(r, 1)
        for c in range(3):
            tiles[r, c : c + 1] = points_here[c, row, :]
            tiles[r, c + 4 : c + 5] = velocity_here[c, row, :]
        tiles[r, 3:4] = mass_here[row, :]
        tiles[r, 7:8] = mass_here[row, :]
        return carry

    lax.fori_loop(0, blocks, gather, 0, unroll=8)
    goal = jnp.broadcast_to(destination_here[...].astype(jnp.float32), (8, blocks))
    fill_points(rows_first, tiles, goal, send)
    meet()

    def one_step(rows, lookup, tiles, send, ghost, thin, density, sems, meanwhile, finish):
        swap_start(send, ghost, *sems[0:2])
        prepare_own(tiles, home, away)
        swap_wait(send, ghost, *sems[0:2])
        prepare_ghosts(blocks, cap, ghost, away)
        sum_densities(lookup, home, away, density, kept, store, store_sem)
        fill_density(rows, density, thin_send)
        swap_start(thin_send, thin, *sems[2:4])
        own_moments(tiles, density, moment, term)
        meanwhile()
        swap_wait(thin_send, thin, *sems[2:4])
        ghost_moments(blocks, ghost, thin, moment)
        sum_forces(lookup, home, away, tiles, moment, term, kept, store, store_sem, finish)

    def finish_first(b, tile, acceleration):
        speed = tile[4:7] + TIME_STEP * acceleration
        place = tile[0:3] + TIME_STEP * speed
        tiles[b] = jnp.concatenate([place, tile[3:4], speed, tile[3:4]], axis=0)

    def finish_second(b, tile, acceleration):
        speed = tile[4:7] + TIME_STEP * acceleration
        place = tile[0:3] + TIME_STEP * speed
        for c in range(3):
            speed_out[c, pl.ds(b, 1), :] = speed[c : c + 1]
            points_out[c, pl.ds(b, 1), :] = place[c : c + 1]

    def plan_moves():
        work_out_moves(destination_here, ghost_first, table, 4 * cap)
        copy = pltpu.make_async_copy(table, table_here, table_sem.at[0])
        copy.start()
        copy.wait()

    one_step(
        rows_first,
        lookup_first_here,
        tiles,
        send,
        ghost_first,
        thin_first,
        density_first,
        pairs[0:4],
        plan_moves,
        finish_first,
    )
    for face in range(6):
        for k in range(MOVE_CAP):
            outbox[face, k] = tiles[table_here[8 * (k + 1) + face, 0]]
    move_blocks(table_here, tiles, moved, outbox, arrived, out_sem, in_sem)
    narrow = send.at[:, pl.ds(0, 4 * cap)]
    fill_points(rows_second, moved, None, narrow)
    one_step(
        rows_second,
        lookup_second_here,
        moved,
        narrow,
        ghost_second,
        thin_second,
        density_out,
        pairs[4:8],
        lambda: None,
        finish_second,
    )


def padded_bytes(shape, dtype):
    *outer, rows, columns = shape
    size = -(-rows // 8) * 8 * -(-columns // 128) * 128 * jnp.dtype(dtype).itemsize
    for dim in outer:
        size *= dim
    return size


def per_device(
    position,
    velocity,
    particle_mass,
    send_first,
    neighbours_first,
    destination,
    send_second,
    neighbours_second,
):
    blocks, _, width = position.shape
    _, devices, cap = send_first.shape
    columns = neighbours_first.shape[1]
    total = blocks + devices * cap
    single, half = jnp.float32, jnp.bfloat16
    turn = lambda a: jnp.transpose(a, (1, 0, 2))
    given = [turn(position), turn(velocity), particle_mass, destination.reshape(1, blocks)]
    outs = [((3, blocks, width), single)] * 2 + [((blocks, width), single)]
    wide = (devices, 4 * cap + 8, width)
    thin = (devices, cap, width)
    box = (6, MOVE_CAP, 8, width)
    fixed = [
        *[(a.shape, a.dtype) for a in given],
        ((blocks, 8, width), single),
        ((blocks, 8, width), single),
        (wide, single),
        ((devices, 4 * cap, width), single),
        (wide, single),
        (thin, single),
        (thin, single),
        (thin, single),
        (box, single),
        (box, single),
        ((blocks, DEPTH, width), half),
        ((total, width, DEPTH), half),
        ((total, 16, width), half),
        ((blocks, width), single),
        ((blocks, width), single),
    ]
    each = padded_bytes((columns + 1, width, width), single)
    left = VMEM_PLAN - sum(padded_bytes(*entry) for entry in fixed + outs)
    kept = max(min(blocks, left // each) // UNROLL, 1) * UNROLL
    weights = (kept, columns + 1, width, width)
    again = min(kept, max(blocks - 2 * kept, 0), SECOND) // UNROLL * UNROLL
    store = (min(kept, blocks - kept) // UNROLL * UNROLL + again, *weights[1:])
    table = (8 * (MOVE_CAP + 1), blocks)
    smem = pl.BlockSpec(memory_space=pltpu.SMEM)
    hbm = pl.BlockSpec(memory_space=pltpu.HBM)
    vmem = pl.BlockSpec(memory_space=pltpu.VMEM)
    lookups = [neighbours_first.T, neighbours_second.T]
    position, velocity, density, _ = pl.pallas_call(
        steps_kernel,
        out_shape=[pltpu.VMEM(*entry) for entry in outs] + [jax.ShapeDtypeStruct(store, single)],
        in_specs=[smem] * 2 + [hbm] * (len(lookups) + len(given)),
        out_specs=[vmem] * len(outs) + [hbm],
        scratch_shapes=[
            *[pltpu.SMEM(a.shape, a.dtype) for a in lookups],
            *[pltpu.VMEM(*entry) for entry in fixed],
            pltpu.VMEM(weights, single),
            pltpu.SemaphoreType.DMA((store[0],)),
            pltpu.VMEM(table, jnp.int32),
            pltpu.SMEM(table, jnp.int32),
            pltpu.SemaphoreType.DMA((len(lookups) + len(given),)),
            pltpu.SemaphoreType.DMA((1,)),
            pltpu.SemaphoreType.DMA((6,)),
            pltpu.SemaphoreType.DMA((6,)),
            *[pltpu.SemaphoreType.DMA((devices,))] * 8,
        ],
        compiler_params=pltpu.CompilerParams(
            vmem_limit_bytes=VMEM_LIMIT, collective_id=0, has_side_effects=True
        ),
    )(
        send_first[0].T,
        send_second[0].T,
        *[pltpu.with_memory_space_constraint(a, pltpu.HBM) for a in lookups + given],
    )
    return turn(position), turn(velocity), density


def solution(mesh):
    whole, flat = P(AXES, None, None), P(AXES, None)
    return jax.shard_map(
        per_device,
        mesh=mesh,
        in_specs=(whole, whole, flat, whole, flat, P(AXES), whole, flat),
        out_specs=(whole, whole, flat),
        check_vma=False,
    )
```
